256 devices in a mesh: ens: 8 (over y, z_hi), tile: 32 (over z_lo, x, core).
Axes of the slice: x: 4, y: 4, z: 8 (z_hi: 2, z_lo: 4; z = z_hi * 4 + z_lo), core: 2. Of those that a mesh axis runs over, the one named last changes fastest.
Arguments:
- fields: bfloat16 [8, 32, 200, 8, 128], P('ens', 'tile'), may hold values from -6 to 6
- target: bfloat16 [8, 32, 200, 8, 128], P('ens', 'tile'), may hold values from -6 to 6
- wet_levels: int32 [32, 8, 128], P('tile'), may hold values from 0 to 19, as said below
- tile_links: int32 [32, 5], replicated, may hold values from -1 to 31, as said below
- tile_owner: int32 [32], replicated, may hold values from 0 to 31, as said below
- kernel: float32 [200, 49], replicated, may hold values from -0.875 to 0.875
- norm_gain: float32 [200], replicated, may hold values from 0.5 to 1.5
- weight_in: bfloat16 [200, 800], replicated, may hold values from -0.4375 to 0.4375
- weight_out: bfloat16 [800, 200], replicated, may hold values from -0.21875 to 0.21875
- layer_scale: float32 [200], replicated, may hold values from 0.25 to 1
Outputs:
- block_out: bfloat16 [8, 32, 200, 8, 128], P('ens', 'tile')
- grad_in: float32 [200, 800], replicated
- grad_out: float32 [800, 200], replicated
- grad_kernel: float32 [200, 49], replicated
The draws below stay inside these ranges and needn't reach their ends.
Inputs may be any that keep to these rules, and one draw needn't show every extreme that they name: `wet_levels`: 0 is land; a cell is wet at the levels below its value. `tile_links`: the kept tiles are the kept blocks of a grid 8 tiles wide, numbered row by row from the south. West and east wrap around within a grid row; the southmost row has no south neighbour; the northmost row is complete, its north neighbour is the tile of the same row in the mirrored column 7 - column, and only it has flag 1 in column 4; -1 marks a missing neighbour. Column 4 is 0 or 1. `tile_owner`: a permutation.
All inputs are finite; a program needn't handle non-finite values.
Results may differ from the reference program's by a relative error of at most 0.005.
Values may be sent and summed in bfloat16 or wider, within the bound.
No kernel may reach another device: no remote copies, remote signals or barrier semaphores. Data moves between devices by JAX's collectives and lax.ppermute only.
A program may use at most 192 MiB of HBM per device.

```python
import math
import jax
import jax.numpy as jnp
from jax import lax

C = 200
HID = 800
TW = 128
TH = 8
LEVELS = 19
TILES = 32
ENS = 8


def draw_wet_levels(key, part):
    key_wet = jax.random.fold_in(key, 11)
    key_depth = jax.random.fold_in(key, 12)
    slot_index = jnp.arange(TILES, dtype=jnp.int32)[:, None, None]
    threshold = 250 + 600 * slot_index // max(TILES - 1, 1)
    scores = jax.random.randint(key_wet, (TILES, TH, TW), 0, 1000)
    depths = jax.random.randint(key_depth, (TILES, TH, TW), 1, LEVELS + 1)
    return jnp.where(scores < threshold, depths, 0).astype(jnp.int32)


def build_links(key):
    grid_rows = TILES // 8 + 1
    grid_cells = grid_rows * 8
    shuffle = jax.random.permutation(jax.random.fold_in(key, 5), TILES)
    dropped = jnp.zeros((TILES,), jnp.int32).at[shuffle[:8]].set(1)
    kept_flag = jnp.concatenate([1 - dropped, jnp.ones((8,), jnp.int32)])
    numbering = jnp.cumsum(kept_flag) - 1
    identity = jnp.where(kept_flag == 1, numbering, -1)
    cell_index = jnp.arange(grid_cells, dtype=jnp.int32)
    row_index = cell_index // 8
    col_index = cell_index % 8
    top_row = row_index == grid_rows - 1
    north_cell = jnp.where(top_row, row_index * 8 + (7 - col_index), cell_index + 8)
    south_cell = jnp.where(row_index == 0, -1, cell_index - 8)
    west_cell = row_index * 8 + (col_index + 7) % 8
    east_cell = row_index * 8 + (col_index + 1) % 8

    def name_of(cells):
        return jnp.where(cells >= 0, identity[jnp.clip(cells, 0, grid_cells - 1)], -1)
    link_table = jnp.stack([name_of(north_cell), name_of(south_cell), name_of(west_cell), name_of(east_cell), top_row.astype(jnp.int32)], axis=1)
    kept_order = jnp.argsort(1 - kept_flag, stable=True)[:TILES]
    return link_table[kept_order].astype(jnp.int32)


def draw_tile_links(key, part):
    return build_links(key)


def draw_tile_owner(key, part):
    links = build_links(key)
    order = jax.random.permutation(jax.random.fold_in(key, 21), TILES).astype(jnp.int32)
    tile_index = jnp.arange(TILES, dtype=jnp.int32)
    usable = (links[:, 3] >= 0) & (links[:, 3] != tile_index)
    first_tile = jnp.argmax(usable).astype(jnp.int32)
    east_tile = jnp.clip(links[first_tile, 3], 0, TILES - 1).astype(jnp.int32)
    wanted = ((order[first_tile] + 1) % TILES).astype(jnp.int32)
    holder = jnp.argmax(order == wanted).astype(jnp.int32)
    east_old = order[east_tile]
    swapped = order.at[holder].set(east_old).at[east_tile].set(wanted)
    return swapped.astype(jnp.int32)


def block_scale(key, dims, cuts, least, largest):
    loudness = 1.0
    for axis_at, blocks in cuts:
        draws = jax.random.uniform(jax.random.fold_in(jax.random.fold_in(key, 6), axis_at), (blocks,), jnp.float32, least / len(cuts), largest / len(cuts))
        loudness = loudness * jnp.repeat(jnp.exp(draws), dims[axis_at] // blocks).reshape((-1,) + (1,) * (len(dims) - 1 - axis_at))
    return loudness


def noise(rng, dims, spread, limit, cuts=(), kind=jnp.bfloat16):
    loudness = block_scale(rng, dims, cuts, -0.22, 0.18) if cuts else 1.0
    entries = jax.random.normal(rng, dims, jnp.float32) * spread * loudness
    return jnp.minimum(jnp.maximum(entries, -limit), limit).astype(kind)


def setup_inputs(seed: int = 0) -> dict:
    key_list = jax.random.split(jax.random.key(seed), 11)
    fields = noise(key_list[0], (ENS, TILES, C, TH, TW), 1.0, 6.0, ((0, 8), (1, 32)))
    target = noise(key_list[1], (ENS, TILES, C, TH, TW), 1.0, 6.0, ((0, 8), (1, 32)))
    wet_levels = draw_wet_levels(jax.random.fold_in(key_list[10], 71), 0)
    tile_links = draw_tile_links(jax.random.fold_in(key_list[10], 71), 0)
    tile_owner = draw_tile_owner(jax.random.fold_in(key_list[10], 71), 0)
    kernel = noise(key_list[5], (C, 49), 49 ** -0.5, 0.875, (), jnp.float32)
    norm_gain = jnp.clip(1.0 + 0.1 * jax.random.normal(key_list[6], (C,), jnp.float32), 0.5, 1.5)
    weight_in = noise(key_list[7], (C, HID), C ** -0.5, 0.4375)
    weight_out = noise(key_list[8], (HID, C), HID ** -0.5, 0.21875)
    layer_scale = jnp.clip(jnp.exp(jax.random.uniform(key_list[9], (C,), jnp.float32, math.log(0.25), math.log(1.0))), 0.25, 1.0)
    return {"fields": fields, "target": target, "wet_levels": wet_levels, "tile_links": tile_links, "tile_owner": tile_owner, "kernel": kernel, "norm_gain": norm_gain, "weight_in": weight_in, "weight_out": weight_out, "layer_scale": layer_scale}


root_half = 0.7071067811865476
gauss_norm = 0.3989422804014327
norm_epsilon = 1e-06

def gelu_value(values):
    return 0.5 * values * (1.0 + lax.erf(values * root_half))

def gelu_slope(values):
    return 0.5 * (1.0 + lax.erf(values * root_half)) + values * jnp.exp(-0.5 * values * values) * gauss_norm

def reference(fields, target, wet_levels, tile_links, tile_owner, kernel, norm_gain, weight_in, weight_out, layer_scale):
    tile_of = jnp.zeros((TILES,), jnp.int32).at[tile_owner].set(jnp.arange(TILES, dtype=jnp.int32))
    level_of = jnp.arange(C, dtype=jnp.int32) * LEVELS // C
    wet_all = wet_levels[:, None, :, :] > level_of[None, :, None, None]
    masked = jnp.where(wet_all[None], fields, jnp.zeros_like(fields))

    def link_of(tile_id, column):
        return jnp.where(tile_id >= 0, tile_links[jnp.clip(tile_id, 0, TILES - 1), column], -1).astype(jnp.int32)

    def tile_at(tile_id):
        slot_id = jnp.where(tile_id >= 0, tile_owner[jnp.clip(tile_id, 0, TILES - 1)], -1).astype(jnp.int32)
        block = lax.dynamic_index_in_dim(masked, jnp.clip(slot_id, 0, TILES - 1), 1, keepdims=False)
        return jnp.where(slot_id >= 0, block, jnp.zeros_like(block))

    def column_tile(tile_id):
        upper_tile = tile_at(link_of(tile_id, 0))
        fold_flag = link_of(tile_id, 4)
        north_rows = jnp.where(fold_flag == 1, jnp.flip(upper_tile[:, :, TH - 3:, :], (2, 3)), upper_tile[:, :, :3, :])
        south_rows = tile_at(link_of(tile_id, 1))[:, :, TH - 3:, :]
        return jnp.concatenate([south_rows, tile_at(tile_id), north_rows], axis=2)
    kernel_wide = kernel.astype(jnp.float32)
    gain_wide = norm_gain.astype(jnp.float32)[None, :, None, None]
    scale_wide = layer_scale.astype(jnp.float32)[None, :, None, None]
    inner_in = weight_in.astype(jnp.float32)
    inner_out = weight_out.astype(jnp.float32)

    def one_slot(slot_id):
        own_tile = tile_of[slot_id]
        center = column_tile(own_tile)
        west_cols = column_tile(link_of(own_tile, 2))[:, :, :, TW - 3:]
        east_cols = column_tile(link_of(own_tile, 3))[:, :, :, :3]
        extended = jnp.concatenate([west_cols, center, east_cols], axis=3).astype(jnp.float32)
        conv_out = jnp.zeros((ENS, C, TH, TW), jnp.float32)
        for row_off in range(7):
            for col_off in range(7):
                conv_out = conv_out + kernel_wide[:, 7 * row_off + col_off][None, :, None, None] * extended[:, :, row_off:row_off + TH, col_off:col_off + TW]
        chan_mean = lax.optimization_barrier(jnp.mean(conv_out, axis=1, keepdims=True))
        chan_var = lax.optimization_barrier(jnp.mean((conv_out - chan_mean) ** 2, axis=1, keepdims=True))
        inv_std = 1.0 / jnp.sqrt(chan_var + norm_epsilon)
        centred = (conv_out - chan_mean) * inv_std
        normed = (centred * gain_wide).astype(jnp.bfloat16)
        flat_norm = normed.reshape(ENS, C, TH * TW).astype(jnp.float32)
        hidden = jnp.einsum('ch,ecp->ehp', inner_in, flat_norm)
        activated = gelu_value(hidden).astype(jnp.bfloat16).astype(jnp.float32)
        mlp_out = jnp.einsum('hc,ehp->ecp', inner_out, activated).reshape(ENS, C, TH, TW)
        own_input = lax.dynamic_index_in_dim(masked, slot_id, 1, keepdims=False).astype(jnp.float32)
        block_out = (own_input + scale_wide * mlp_out).astype(jnp.bfloat16)
        wet_mask = wet_all[slot_id]
        own_target = lax.dynamic_index_in_dim(target, slot_id, 1, keepdims=False).astype(jnp.float32)
        misfit = jnp.where(wet_mask[None], block_out.astype(jnp.float32) - own_target, 0.0)
        grad_mlp = (2.0 * scale_wide * misfit).astype(jnp.bfloat16).reshape(ENS, C, TH * TW).astype(jnp.float32)
        part_out = jnp.einsum('ehp,ecp->hc', activated, grad_mlp)
        grad_act = jnp.einsum('hc,ecp->ehp', inner_out, grad_mlp)
        grad_hidden = (grad_act * gelu_slope(hidden)).astype(jnp.bfloat16).astype(jnp.float32)
        part_in = jnp.einsum('ecp,ehp->ch', flat_norm, grad_hidden)
        grad_normed = jnp.einsum('ch,ehp->ecp', inner_in, grad_hidden).reshape(ENS, C, TH, TW)
        grad_scaled = grad_normed * gain_wide
        grad_conv = (grad_scaled - lax.optimization_barrier(jnp.mean(grad_scaled, axis=1, keepdims=True)) - centred * lax.optimization_barrier(jnp.mean(grad_scaled * centred, axis=1, keepdims=True))) * inv_std
        kernel_terms = []
        for row_off in range(7):
            for col_off in range(7):
                kernel_terms.append(lax.optimization_barrier(jnp.sum(grad_conv * extended[:, :, row_off:row_off + TH, col_off:col_off + TW], axis=(0, 2, 3))))
        part_kernel = jnp.stack(kernel_terms, axis=1)
        return (block_out, part_in, part_out, part_kernel)
    outputs, part_in, part_out, part_kernel = lax.map(one_slot, jnp.arange(TILES, dtype=jnp.int32))
    entry_total = jnp.float32(ENS * TILES * C * TH * TW)
    block_out = jnp.swapaxes(outputs, 0, 1)
    return (block_out, lax.optimization_barrier(jnp.sum(part_in, axis=0)) / entry_total, lax.optimization_barrier(jnp.sum(part_out, axis=0)) / entry_total, lax.optimization_barrier(jnp.sum(part_kernel, axis=0)) / entry_total)
```

```python
import jax
import jax.numpy as jnp
from jax import lax
from jax.experimental import pallas as pl
from jax.experimental.pallas import tpu as pltpu
from jax.sharding import PartitionSpec as P

LEVELS = 19
TILES = 32
CH = 200
PARTS = 7
ROWS = 8
COLS = 128
EXT = 14
TAPS = 7
HID = 800
CELLS = ROWS * COLS
CHUNKS = 32
SUB = 12

root_half = 0.7071067811865476
gauss_norm = 0.3989422804014327
norm_epsilon = 1e-06
f32 = jnp.float32
bf16 = jnp.bfloat16
AXES = ("ens", "tile")
BIG = 48 << 20


def gelu_value(values):
    return 0.5 * values * (1.0 + lax.erf(values * root_half))


def gelu_slope(values):
    return (
        0.5 * (1.0 + lax.erf(values * root_half))
        + values * jnp.exp(-0.5 * values * values) * gauss_norm
    )


def link_at(links, tile_id, column):
    return jnp.where(tile_id >= 0, links[jnp.maximum(tile_id, 0), column], -1)


def compose_kernel(links, owner, x_ref, o_ref, inverse):
    shape = (PARTS, ROWS, COLS)
    row = lax.broadcasted_iota(jnp.int32, shape, 1)
    lane = lax.broadcasted_iota(jnp.int32, shape, 2)
    edge = (lane < 3) | (lane >= COLS - 3)
    east_side = lane < 64

    def note(k, _):
        inverse[owner[k]] = k
        return 0

    lax.fori_loop(0, TILES, note, 0)

    def load(tile_id):
        slot = jnp.where(tile_id >= 0, owner[jnp.maximum(tile_id, 0)], 0)
        block = x_ref[slot].astype(f32)
        return jnp.where(tile_id >= 0, block, 0.0)

    def north_of(tile_id):
        block = load(link_at(links, tile_id, 0))
        return jnp.where(link_at(links, tile_id, 4) == 1, pltpu.roll(block, 3, 1), block)

    def body(d, _):
        own = inverse[d]
        west = link_at(links, own, 2)
        east = link_at(links, own, 3)
        north_rows = north_of(own)
        south_rows = load(link_at(links, own, 1))
        sides = jnp.where(edge, jnp.where(east_side, load(east), load(west)), 0.0)
        north_side = (lane < 64) != (link_at(links, own, 4) == 1)
        north_corner = jnp.where(north_side, north_of(east), north_of(west))
        south_corner = jnp.where(
            east_side, load(link_at(links, east, 1)), load(link_at(links, west, 1))
        )
        corners = jnp.where(row < 3, north_corner, south_corner)
        corners = jnp.where(edge & ((row < 3) | (row > 4)), corners, 0.0)
        spread = pltpu.roll(
            sides + pltpu.roll(corners, 64, 2), 24, 2, stride=8, stride_axis=1
        )
        packed = jnp.sum(spread, axis=1, keepdims=True)
        block = jnp.where(row == 3, packed, jnp.where(row < 3, north_rows, south_rows))
        o_ref[d] = block.astype(bf16)
        return 0

    lax.fori_loop(0, TILES, body, 0)


def compose(links, owner, chunks):
    smem = pl.BlockSpec(memory_space=pltpu.SMEM)
    vmem = pl.BlockSpec(memory_space=pltpu.VMEM)
    return pl.pallas_call(
        compose_kernel,
        out_shape=jax.ShapeDtypeStruct((TILES, PARTS, ROWS, COLS), bf16),
        in_specs=[smem, smem, vmem],
        out_specs=vmem,
        scratch_shapes=[pltpu.SMEM((TILES,), jnp.int32)],
        compiler_params=pltpu.CompilerParams(vmem_limit_bytes=BIG),
        name="compose",
    )(links, owner, chunks)


def shifted(center, halo, col_off, lane):
    if col_off < 3:
        k = 3 - col_off
        return pltpu.roll(jnp.where(lane >= COLS - k, halo, center), k, 1)
    if col_off > 3:
        k = col_off - 3
        return pltpu.roll(jnp.where(lane < k, halo, center), COLS - k, 1)
    return center


def conv_kernel(
    links, owner, own_slot, m_ref, r_ref, coef, cen_ref, norm_ref, inv_ref, ext, halo, flat_ref, mine, rims
):
    slot = own_slot[0]

    def find(k, best):
        return jnp.where(owner[k] == slot, k, best)

    own = lax.fori_loop(0, TILES, find, 0)
    fold = links[own, 4] == 1
    mine[...] = m_ref[0:CH].astype(f32).reshape(CH * ROWS, COLS)
    rims[...] = r_ref[0:CH].astype(f32).reshape(CH * ROWS, COLS)
    for r in range(ROWS):
        values = mine[pl.ds(r, CH, stride=ROWS), :]
        ext[3 + r] = values
        flat_ref[:, COLS * r : COLS * r + COLS] = values.astype(bf16)
    row = lax.broadcasted_iota(jnp.int32, (COLS, COLS), 0)
    col = lax.broadcasted_iota(jnp.int32, (COLS, COLS), 1)
    turn = (row == jnp.where(fold, COLS - 1 - col, col)).astype(f32).astype(bf16)
    edges = rims[pl.ds(3, CH, stride=ROWS), :]
    for r in range(11):
        halo[r] = edges if r == 0 else pltpu.roll(edges, COLS - 8 * r, 1)
    north = [rims[pl.ds(t, CH, stride=ROWS), :] for t in range(3)]
    corner = [pltpu.roll(edges, COLS - 8 * (11 + t), 1) for t in range(3)]
    for t in range(3):
        ext[t] = rims[pl.ds(5 + t, CH, stride=ROWS), :]
        for dest, source in ((ext, north), (halo, corner)):
            raw = jnp.where(fold, source[2 - t], source[t]).astype(bf16)
            dest[11 + t] = jnp.dot(raw, turn, preferred_element_type=f32)
    lane = lax.broadcasted_iota(jnp.int32, (8, COLS), 1)

    def block(i, sums):
        at = pl.ds(pl.multiple_of(8 * i, 8), 8)
        taps = coef[at, :]
        acc = [jnp.zeros((8, COLS), f32) for _ in range(ROWS)]
        for b in range(TAPS):
            moved = [shifted(ext[r, at, :], halo[r, at, :], b, lane) for r in range(EXT)]
            for a in range(TAPS):
                tap = jnp.broadcast_to(taps[:, 7 * a + b : 7 * a + b + 1], (8, COLS))
                for r in range(ROWS):
                    acc[r] = acc[r] + tap * moved[r + a]
        for r in range(ROWS):
            cen_ref[at, COLS * r : COLS * r + COLS] = acc[r]
        return tuple(s + x for s, x in zip(sums, acc))

    sums = lax.fori_loop(0, CH // 8, block, tuple(jnp.zeros((8, COLS), f32) for _ in range(ROWS)))
    gain = jnp.broadcast_to(coef[:, 49:50], (CH, COLS))
    for r in range(ROWS):
        at = slice(COLS * r, COLS * r + COLS)
        mean = jnp.sum(sums[r], axis=0, keepdims=True) * (1.0 / CH)
        off = cen_ref[:, at] - mean
        var = jnp.sum(off * off, axis=0, keepdims=True) * (1.0 / CH)
        inv = 1.0 / jnp.sqrt(var + norm_epsilon)
        centred = off * inv
        cen_ref[:, at] = centred
        norm_ref[:, at] = (centred * gain).astype(bf16)
        inv_ref[r : r + 1, :] = inv


def forward_conv(links, owner, own_slot, payload, rims, coef):
    smem = pl.BlockSpec(memory_space=pltpu.SMEM)
    vmem = pl.BlockSpec(memory_space=pltpu.VMEM)
    shapes = [
        ((CH, CELLS), f32),
        ((CH, CELLS), bf16),
        ((ROWS, COLS), f32),
        ((EXT, CH, COLS), f32),
        ((EXT, CH, COLS), f32),
        ((CH, CELLS), bf16),
    ]
    return pl.pallas_call(
        conv_kernel,
        out_shape=[jax.ShapeDtypeStruct(s, d) for s, d in shapes],
        in_specs=[smem, smem, smem, vmem, vmem, vmem],
        out_specs=[vmem] * len(shapes),
        scratch_shapes=[pltpu.VMEM((CH * ROWS, COLS), f32)] * 2,
        compiler_params=pltpu.CompilerParams(vmem_limit_bytes=BIG),
        name="forward_conv",
    )(links, owner, own_slot, payload, rims, coef)


def grad_kernel(me, gn_ref, cen_ref, inv_ref, ext, halo, coef, in_ref, out_ref, keep, send, gconv, pack):
    gain = jnp.broadcast_to(coef[:, 49:50], (CH, COLS))
    for r in range(ROWS):
        at = slice(COLS * r, COLS * r + COLS)
        scaled = gn_ref[:, at] * gain
        centred = cen_ref[:, at]
        mean = jnp.sum(scaled, axis=0, keepdims=True) * (1.0 / CH)
        along = jnp.sum(scaled * centred, axis=0, keepdims=True) * (1.0 / CH)
        gconv[:, at] = (scaled - mean - centred * along) * inv_ref[r : r + 1, :]
    lane = lax.broadcasted_iota(jnp.int32, (8, COLS), 1)

    def block(i, _):
        at = pl.ds(pl.multiple_of(8 * i, 8), 8)
        grads = [gconv[at, COLS * r : COLS * r + COLS] for r in range(ROWS)]
        found = jnp.zeros((8, COLS), f32)
        for b in range(TAPS):
            moved = [shifted(ext[r, at, :], halo[r, at, :], b, lane) for r in range(EXT)]
            for a in range(TAPS):
                terms = grads[0] * moved[a]
                for r in range(1, ROWS):
                    terms = terms + grads[r] * moved[r + a]
                total = jnp.sum(terms, axis=1, keepdims=True)
                found = jnp.where(lane == 32 + 7 * a + b, total, found)
        for t in range(6):
            pack[7 * i + t] = in_ref[at, COLS * t : COLS * t + COLS]
        tail = jnp.concatenate([in_ref[at, 6 * COLS : HID], jnp.zeros((8, 96), f32)], axis=1)
        pack[7 * i + 6] = jnp.where(lane < 32, tail, found)
        return 0

    lax.fori_loop(0, CH // 8, block, 0)

    def rows(i, _):
        at = pl.ds(pl.multiple_of(8 * i, 8), 8)
        pack[175 + 2 * i] = out_ref[at, 0:COLS]
        pack[176 + 2 * i] = jnp.concatenate(
            [out_ref[at, COLS:CH], jnp.zeros((8, 2 * COLS - CH), f32)], axis=1
        )
        return 0

    lax.fori_loop(0, HID // 8, rows, 0)
    for t in range(375, CHUNKS * SUB):
        pack[t] = jnp.zeros((8, COLS), f32)

    def split(j, _):
        for dest, offset in ((keep, 0), (send, 16)):
            source = ((j + offset) ^ me[0]) * SUB
            for t in range(SUB):
                dest[j, 8 * t : 8 * t + 8, :] = pack[source + t]
        return 0

    lax.fori_loop(0, CHUNKS // 2, split, 0)


def backward_conv(me, gn, cen, inv, ext, halo, coef, part_in, part_out):
    smem = pl.BlockSpec(memory_space=pltpu.SMEM)
    vmem = pl.BlockSpec(memory_space=pltpu.VMEM)
    half = jax.ShapeDtypeStruct((CHUNKS // 2, 8 * SUB, COLS), f32)
    return pl.pallas_call(
        grad_kernel,
        out_shape=[half, half],
        in_specs=[smem] + [vmem] * 8,
        out_specs=[vmem, vmem],
        scratch_shapes=[
            pltpu.VMEM((CH, CELLS), f32),
            pltpu.VMEM((CHUNKS * SUB, 8, COLS), f32),
        ],
        compiler_params=pltpu.CompilerParams(vmem_limit_bytes=BIG),
        name="backward_conv",
    )(me, gn, cen, inv, ext, halo, coef, part_in, part_out)


def unpack_kernel(me, x_ref, in_ref, out_ref, k_ref, pack):
    share = 1.0 / (8 * TILES * CH * CELLS)

    def order(j, _):
        dest = (j ^ me[0]) * SUB
        values = x_ref[j].astype(f32) * share
        for t in range(SUB):
            pack[dest + t] = values[8 * t : 8 * t + 8, :]
        return 0

    lax.fori_loop(0, CHUNKS, order, 0)

    def block(i, _):
        at = pl.ds(pl.multiple_of(8 * i, 8), 8)
        for t in range(6):
            in_ref[at, COLS * t : COLS * t + COLS] = pack[7 * i + t]
        tail = pack[7 * i + 6]
        in_ref[at, 6 * COLS : HID] = tail[:, 0:32]
        k_ref[at, :] = tail[:, 32:81]
        return 0

    lax.fori_loop(0, CH // 8, block, 0)

    def rows(i, _):
        at = pl.ds(pl.multiple_of(8 * i, 8), 8)
        out_ref[at, 0:COLS] = pack[175 + 2 * i]
        out_ref[at, COLS:CH] = pack[176 + 2 * i][:, 0 : CH - COLS]
        return 0

    lax.fori_loop(0, HID // 8, rows, 0)


def unpack(me, gathered):
    vmem = pl.BlockSpec(memory_space=pltpu.VMEM)
    return pl.pallas_call(
        unpack_kernel,
        out_shape=[
            jax.ShapeDtypeStruct((CH, HID), f32),
            jax.ShapeDtypeStruct((HID, CH), f32),
            jax.ShapeDtypeStruct((CH, 49), f32),
        ],
        in_specs=[pl.BlockSpec(memory_space=pltpu.SMEM), vmem],
        out_specs=[vmem] * 3,
        scratch_shapes=[pltpu.VMEM((CHUNKS * SUB, 8, COLS), f32)],
        compiler_params=pltpu.CompilerParams(vmem_limit_bytes=BIG),
        name="unpack",
    )(me, gathered)


def swap(values, bits):
    return lax.ppermute(values, AXES, [(i, i ^ bits) for i in range(256)])


def reduce_all(keep, send):
    held = keep + swap(send, 1)
    held = held.reshape(4, 4, 8 * SUB, COLS)
    held = (held[0] + swap(held[1], 2)) + (swap(held[2], 4) + swap(held[3], 6))
    held = (held[0] + swap(held[1], 64)) + (swap(held[2], 128) + swap(held[3], 192))
    for bits in (8, 16, 32):
        held = held + swap(held, bits)
    part = held.astype(bf16)
    part = jnp.stack([part] + [swap(part, k << 6) for k in (1, 2, 3)])
    part = jnp.stack([part] + [swap(part, k << 1) for k in (1, 2, 3)])
    part = jnp.stack([part, swap(part, 1)])
    return part.reshape(CHUNKS, 8 * SUB, COLS)


def local(
    fields,
    target,
    wet_levels,
    tile_links,
    tile_owner,
    kernel,
    norm_gain,
    weight_in,
    weight_out,
    layer_scale,
):
    tile_at = lax.axis_index("tile").astype(jnp.int32)
    ens_at = lax.axis_index("ens").astype(jnp.int32)
    own_slot = tile_at.reshape(1)
    me = ((tile_at & 1) * 16 + ((tile_at >> 1) & 3) * 4 + (ens_at >> 1)).reshape(1)
    level_of = jnp.arange(CH, dtype=jnp.int32) * LEVELS // CH
    wet_mask = wet_levels[0][None, :, :] > level_of[:, None, None]
    own_input = fields[0, 0]
    masked = jnp.where(wet_mask, own_input, jnp.zeros_like(own_input))
    payload = jnp.pad(masked, ((0, TILES * PARTS - CH), (0, 0), (0, 0)))
    coef = jnp.concatenate([kernel, norm_gain[:, None], layer_scale[:, None]], axis=1)

    chunks = lax.all_to_all(
        payload.reshape(TILES, PARTS, ROWS, COLS), "tile", 0, 0, tiled=True
    )
    rims = lax.all_to_all(compose(tile_links, tile_owner, chunks), "tile", 0, 0, tiled=True)
    rims = rims.reshape(TILES * PARTS, ROWS, COLS)
    centred, flat_norm, inv_std, ext, halo, flat_masked = forward_conv(
        tile_links, tile_owner, own_slot, payload, rims, coef
    )

    scale_wide = layer_scale[:, None]
    hidden = jnp.einsum("ch,cp->hp", weight_in, flat_norm, preferred_element_type=f32)
    activated = gelu_value(hidden).astype(bf16)
    mlp_out = jnp.einsum("hc,hp->cp", weight_out, activated, preferred_element_type=f32)
    block_out = (flat_masked.astype(f32) + scale_wide * mlp_out).astype(bf16)
    flat_wet = wet_levels[0].reshape(1, CELLS) > level_of[:, None]
    misfit = jnp.where(
        flat_wet, block_out.astype(f32) - target[0, 0].reshape(CH, CELLS).astype(f32), 0.0
    )
    grad_mlp = (2.0 * scale_wide * misfit).astype(bf16)
    part_out = jnp.einsum("hp,cp->hc", activated, grad_mlp, preferred_element_type=f32)
    grad_act = jnp.einsum("hc,cp->hp", weight_out, grad_mlp, preferred_element_type=f32)
    grad_hidden = (grad_act * gelu_slope(hidden)).astype(bf16)
    part_in = jnp.einsum("cp,hp->ch", flat_norm, grad_hidden, preferred_element_type=f32)
    grad_normed = jnp.einsum("ch,hp->cp", weight_in, grad_hidden, preferred_element_type=f32)

    keep, send = backward_conv(
        me, grad_normed, centred, inv_std, ext, halo, coef, part_in, part_out
    )
    grad_in, grad_out, grad_taps = unpack(me, reduce_all(keep, send))
    return block_out.reshape(1, 1, CH, ROWS, COLS), grad_in, grad_out, grad_taps


def solution(mesh):
    placed = (
        P("ens", "tile", None, None, None),
        P("ens", "tile", None, None, None),
        P("tile", None, None),
        P(),
        P(),
        P(),
        P(),
        P(),
        P(),
        P(),
    )
    return jax.shard_map(
        local,
        mesh=mesh,
        in_specs=placed,
        out_specs=(P("ens", "tile", None, None, None), P(), P(), P()),
        check_vma=False,
    )
```

```python
import jax
import jax.numpy as jnp
from jax import lax
from jax.experimental import pallas as pl
from jax.experimental.pallas import tpu as pltpu
from jax.sharding import PartitionSpec as P

LEVELS = 19
TILES = 32
CH = 200
PARTS = 7
ROWS = 8
COLS = 128
EXT = 14
TAPS = 7
HID = 800
CELLS = ROWS * COLS
CHUNKS = 32
SUB = 11
TILES_IN = 175

root_half = 0.7071067811865476
gauss_norm = 0.3989422804014327
norm_epsilon = 1e-06
f32 = jnp.float32
bf16 = jnp.bfloat16
AXES = ("ens", "tile")
BIG = 24 << 20


def gelu_value(values):
    return 0.5 * values * (1.0 + lax.erf(values * root_half))


def gelu_slope(values):
    return (
        0.5 * (1.0 + lax.erf(values * root_half))
        + values * jnp.exp(-0.5 * values * values) * gauss_norm
    )


def link_at(links, tile_id, column):
    return jnp.where(tile_id >= 0, links[jnp.maximum(tile_id, 0), column], -1)


def compose_kernel(links, owner, x_ref, o_ref, inverse):
    shape = (PARTS, ROWS, COLS)
    row = lax.broadcasted_iota(jnp.int32, shape, 1)
    lane = lax.broadcasted_iota(jnp.int32, shape, 2)
    edge = (lane < 3) | (lane >= COLS - 3)
    east_side = lane < 64

    def note(k, _):
        inverse[owner[k]] = k
        return 0

    lax.fori_loop(0, TILES, note, 0)

    def load(tile_id):
        slot = jnp.where(tile_id >= 0, owner[jnp.maximum(tile_id, 0)], 0)
        block = x_ref[slot].astype(f32)
        return jnp.where(tile_id >= 0, block, 0.0)

    def north_of(tile_id):
        block = load(link_at(links, tile_id, 0))
        return jnp.where(link_at(links, tile_id, 4) == 1, pltpu.roll(block, 3, 1), block)

    def body(d, _):
        own = inverse[d]
        west = link_at(links, own, 2)
        east = link_at(links, own, 3)
        north_rows = north_of(own)
        south_rows = load(link_at(links, own, 1))
        sides = jnp.where(edge, jnp.where(east_side, load(east), load(west)), 0.0)
        north_side = (lane < 64) != (link_at(links, own, 4) == 1)
        north_corner = jnp.where(north_side, north_of(east), north_of(west))
        south_corner = jnp.where(
            east_side, load(link_at(links, east, 1)), load(link_at(links, west, 1))
        )
        corners = jnp.where(row < 3, north_corner, south_corner)
        corners = jnp.where(edge & ((row < 3) | (row > 4)), corners, 0.0)
        spread = pltpu.roll(
            sides + pltpu.roll(corners, 64, 2), 24, 2, stride=8, stride_axis=1
        )
        packed = jnp.sum(spread, axis=1, keepdims=True)
        block = jnp.where(row == 3, packed, jnp.where(row < 3, north_rows, south_rows))
        o_ref[d] = block.astype(bf16)
        return 0

    lax.fori_loop(0, TILES, body, 0, unroll=8)


def compose(links, owner, chunks):
    smem = pl.BlockSpec(memory_space=pltpu.SMEM)
    vmem = pl.BlockSpec(memory_space=pltpu.VMEM)
    return pl.pallas_call(
        compose_kernel,
        out_shape=jax.ShapeDtypeStruct((TILES, PARTS, ROWS, COLS), bf16),
        in_specs=[smem, smem, vmem],
        out_specs=vmem,
        scratch_shapes=[pltpu.SMEM((TILES,), jnp.int32)],
        compiler_params=pltpu.CompilerParams(vmem_limit_bytes=BIG),
        name="compose",
    )(links, owner, chunks)


def chosen(center, halo, col_off, lane):
    if col_off < 3:
        return jnp.where(lane >= COLS - 3 + col_off, halo, center)
    if col_off > 3:
        return jnp.where(lane < col_off - 3, halo, center)
    return center


def turned(values, col_off):
    return values if col_off == 3 else pltpu.roll(values, (3 - col_off) % COLS, 1)


def extended_rows(own_rows, ext, halo, at, col_off, lane):
    rows = [ext[r, at, :] for r in range(3)]
    rows += [own_rows[r, at, :] for r in range(ROWS)]
    rows += [ext[r, at, :] for r in range(3, 6)]
    return [chosen(x, halo[r, at, :], col_off, lane) for r, x in enumerate(rows)]


def prepare_kernel(m_ref, coef, own, wide, flat_ref, mine):
    mine[...] = m_ref[0:CH].astype(f32).reshape(CH * ROWS, COLS)
    for r in range(ROWS):
        values = mine[pl.ds(r, CH, stride=ROWS), :]
        own[r] = values
        flat_ref[:, COLS * r : COLS * r + COLS] = values.astype(bf16)
    for k in range(TAPS * TAPS):
        wide[k] = jnp.broadcast_to(coef[:, k : k + 1], (CH, COLS))


def prepare(payload, coef):
    vmem = pl.BlockSpec(memory_space=pltpu.VMEM)
    return pl.pallas_call(
        prepare_kernel,
        out_shape=[
            jax.ShapeDtypeStruct((ROWS, CH, COLS), f32),
            jax.ShapeDtypeStruct((TAPS * TAPS, CH, COLS), f32),
            jax.ShapeDtypeStruct((CH, CELLS), bf16),
        ],
        in_specs=[vmem, vmem],
        out_specs=[vmem] * 3,
        scratch_shapes=[pltpu.VMEM((CH * ROWS, COLS), f32)],
        compiler_params=pltpu.CompilerParams(vmem_limit_bytes=BIG),
        name="prepare",
    )(payload, coef)


def conv_kernel(
    links, owner, own_slot, own_rows, taps, r_ref, coef, cen_ref, norm_ref, inv_ref, ext, halo, rims, wide, arrived
):
    fetch = pltpu.make_async_copy(taps, wide, arrived)
    fetch.start()
    slot = own_slot[0]

    def find(k, best):
        return jnp.where(owner[k] == slot, k, best)

    own = lax.fori_loop(0, TILES, find, 0)
    fold = links[own, 4] == 1
    rims[...] = r_ref[0:CH].astype(f32).reshape(CH * ROWS, COLS)
    row = lax.broadcasted_iota(jnp.int32, (COLS, COLS), 0)
    col = lax.broadcasted_iota(jnp.int32, (COLS, COLS), 1)
    turn = (row == jnp.where(fold, COLS - 1 - col, col)).astype(f32).astype(bf16)
    edges = rims[pl.ds(3, CH, stride=ROWS), :]
    for r in range(11):
        halo[r] = edges if r == 0 else pltpu.roll(edges, COLS - 8 * r, 1)
    north = [rims[pl.ds(t, CH, stride=ROWS), :] for t in range(3)]
    corner = [pltpu.roll(edges, COLS - 8 * (11 + t), 1) for t in range(3)]
    for t in range(3):
        ext[t] = rims[pl.ds(5 + t, CH, stride=ROWS), :]
        for dest, source, first in ((ext, north, 3), (halo, corner, 11)):
            raw = jnp.where(fold, source[2 - t], source[t]).astype(bf16)
            dest[first + t] = jnp.dot(raw, turn, preferred_element_type=f32)
    lane = lax.broadcasted_iota(jnp.int32, (8, COLS), 1)
    fetch.wait()

    def block(i, sums):
        at = pl.ds(pl.multiple_of(8 * i, 8), 8)
        acc = [jnp.zeros((8, COLS), f32) for _ in range(ROWS)]
        for b in range(TAPS):
            moved = extended_rows(own_rows, ext, halo, at, b, lane)
            part = [None] * ROWS
            for a in range(TAPS):
                tap = wide[7 * a + b, at, :]
                for r in range(ROWS):
                    term = tap * moved[r + a]
                    part[r] = term if a == 0 else part[r] + term
            for r in range(ROWS):
                acc[r] = acc[r] + turned(part[r], b)
        for r in range(ROWS):
            cen_ref[at, COLS * r : COLS * r + COLS] = acc[r]
        return tuple(s + x for s, x in zip(sums, acc))

    sums = lax.fori_loop(0, CH // 8, block, tuple(jnp.zeros((8, COLS), f32) for _ in range(ROWS)))
    gain = jnp.broadcast_to(coef[:, 49:50], (CH, COLS))
    for r in range(ROWS):
        at = slice(COLS * r, COLS * r + COLS)
        mean = jnp.sum(sums[r], axis=0, keepdims=True) * (1.0 / CH)
        off = cen_ref[:, at] - mean
        var = jnp.sum(off * off, axis=0, keepdims=True) * (1.0 / CH)
        inv = 1.0 / jnp.sqrt(var + norm_epsilon)
        centred = off * inv
        cen_ref[:, at] = centred
        norm_ref[:, at] = (centred * gain).astype(bf16)
        inv_ref[r : r + 1, :] = inv


def forward_conv(links, owner, own_slot, own_rows, wide, rims, coef):
    smem = pl.BlockSpec(memory_space=pltpu.SMEM)
    vmem = pl.BlockSpec(memory_space=pltpu.VMEM)
    shapes = [
        ((CH, CELLS), f32),
        ((CH, CELLS), bf16),
        ((ROWS, COLS), f32),
        ((6, CH, COLS), f32),
        ((EXT, CH, COLS), f32),
    ]
    return pl.pallas_call(
        conv_kernel,
        out_shape=[jax.ShapeDtypeStruct(s, d) for s, d in shapes],
        in_specs=[smem, smem, smem, vmem, pl.BlockSpec(memory_space=pl.ANY), vmem, vmem],
        out_specs=[vmem] * len(shapes),
        scratch_shapes=[
            pltpu.VMEM((CH * ROWS, COLS), f32),
            pltpu.VMEM((TAPS * TAPS, CH, COLS), f32),
            pltpu.SemaphoreType.DMA,
        ],
        compiler_params=pltpu.CompilerParams(vmem_limit_bytes=BIG),
        name="forward_conv",
    )(links, owner, own_slot, own_rows, wide, rims, coef)


def grad_kernel(
    me, gn_ref, cen_ref, inv_ref, own_rows, ext, halo, coef, in_ref, out_ref, packed, gconv, terms_ref
):
    gain = jnp.broadcast_to(coef[:, 49:50], (CH, COLS))
    for r in range(ROWS):
        at = slice(COLS * r, COLS * r + COLS)
        scaled = gn_ref[:, at] * gain
        centred = cen_ref[:, at]
        mean = jnp.sum(scaled, axis=0, keepdims=True) * (1.0 / CH)
        along = jnp.sum(scaled * centred, axis=0, keepdims=True) * (1.0 / CH)
        gconv[:, at] = (scaled - mean - centred * along) * inv_ref[r : r + 1, :]
    lane = lax.broadcasted_iota(jnp.int32, (8, COLS), 1)

    def block(i, _):
        at = pl.ds(pl.multiple_of(8 * i, 8), 8)
        grads = [gconv[at, COLS * r : COLS * r + COLS] for r in range(ROWS)]
        for b in range(TAPS):
            moved = extended_rows(own_rows, ext, halo, at, b, lane)
            back = [turned(g, 6 - b) for g in grads]
            for a in range(TAPS):
                terms = back[0] * moved[a]
                for r in range(1, ROWS):
                    terms = terms + back[r] * moved[r + a]
                terms_ref[7 * a + b, at, :] = terms
        return 0

    lax.fori_loop(0, CH // 8, block, 0)
    ones = jnp.ones((COLS, COLS), bf16)
    wide_lane = lax.broadcasted_iota(jnp.int32, (CH, COLS), 1)
    found = jnp.zeros((CH, COLS), f32)
    for k in range(TAPS * TAPS):
        terms = terms_ref[k]
        high = terms.astype(bf16)
        low = (terms - high.astype(f32)).astype(bf16)
        total = jnp.dot(high, ones, preferred_element_type=f32)
        total = total + jnp.dot(low, ones, preferred_element_type=f32)
        found = jnp.where(wide_lane == 32 + k, total, found)
    place = [chunk ^ me[0] for chunk in range(CHUNKS)]
    blank = jnp.zeros((8, 96), f32)
    for t in range(CHUNKS * SUB):
        source, at = (in_ref, t) if t < TILES_IN else (out_ref, t - TILES_IN)
        i, l = at // 7, at % 7
        if i >= CH // 8:
            tile = jnp.zeros((8, COLS), f32)
        elif l < 6:
            tile = source[8 * i : 8 * i + 8, COLS * l : COLS * l + COLS]
        else:
            tile = jnp.concatenate([source[8 * i : 8 * i + 8, 6 * COLS : HID], blank], axis=1)
            if t < TILES_IN:
                tile = jnp.where(lane < 32, tile, found[8 * i : 8 * i + 8, :])
        at = 8 * (t % SUB)
        packed[place[t // SUB], at : at + 8, :] = tile


def backward_conv(me, gn, cen, inv, own_rows, ext, halo, coef, part_in, part_out):
    smem = pl.BlockSpec(memory_space=pltpu.SMEM)
    vmem = pl.BlockSpec(memory_space=pltpu.VMEM)
    return pl.pallas_call(
        grad_kernel,
        out_shape=jax.ShapeDtypeStruct((CHUNKS, 8 * SUB, COLS), f32),
        in_specs=[smem] + [vmem] * 9,
        out_specs=vmem,
        scratch_shapes=[
            pltpu.VMEM((CH, CELLS), f32),
            pltpu.VMEM((TAPS * TAPS, CH, COLS), f32),
        ],
        compiler_params=pltpu.CompilerParams(vmem_limit_bytes=BIG),
        name="backward_conv",
    )(me, gn, cen, inv, own_rows, ext, halo, coef, part_in, part_out)


def unpack_kernel(me, x_ref, in_ref, out_ref, k_ref, taps):
    share = 1.0 / (8 * TILES * CH * CELLS)
    for chunk in range(CHUNKS):
        values = x_ref[chunk ^ me[0]].astype(f32) * share
        for p in range(SUB):
            t = SUB * chunk + p
            dest, at = (in_ref, t) if t < TILES_IN else (out_ref, t - TILES_IN)
            i, l = at // 7, at % 7
            tile = values[8 * p : 8 * p + 8, :]
            if i >= CH // 8:
                continue
            if l < 6:
                dest[8 * i : 8 * i + 8, COLS * l : COLS * l + COLS] = tile
            else:
                dest[8 * i : 8 * i + 8, 6 * COLS : HID] = tile[:, 0:32]
                if t < TILES_IN:
                    taps[8 * i : 8 * i + 8, :] = tile
    taps[CH:256, :] = jnp.zeros((256 - CH, COLS), f32)
    k_ref[...] = jnp.transpose(taps[...])[32:81, 0:CH]


def unpack(me, gathered):
    vmem = pl.BlockSpec(memory_space=pltpu.VMEM)
    return pl.pallas_call(
        unpack_kernel,
        out_shape=[
            jax.ShapeDtypeStruct((CH, HID), f32),
            jax.ShapeDtypeStruct((CH, HID), f32),
            jax.ShapeDtypeStruct((49, CH), f32),
        ],
        in_specs=[pl.BlockSpec(memory_space=pltpu.SMEM), vmem],
        out_specs=[vmem] * 3,
        scratch_shapes=[pltpu.VMEM((256, COLS), f32)],
        compiler_params=pltpu.CompilerParams(vmem_limit_bytes=BIG),
        name="unpack",
    )(me, gathered)


def swap(values, bits):
    return lax.ppermute(values, AXES, [(i, i ^ bits) for i in range(256)])


def reduce_all(held):
    held = (held[:16] + swap(held[16:], 1)).reshape(4, 4, 8 * SUB, COLS)
    sent = [swap(held[k].astype(bf16), k << 1).astype(f32) for k in (1, 2, 3)]
    held = (held[0] + sent[0]) + (sent[1] + sent[2])
    held = (held[0] + swap(held[1], 64)) + (swap(held[2], 128) + swap(held[3], 192))
    held = (held + swap(held, 8)) + (swap(held, 16) + swap(held, 24))
    held = held + swap(held, 32)
    part = held.astype(bf16)
    part = jnp.stack([part] + [swap(part, k << 6) for k in (1, 2, 3)])
    part = jnp.stack([part] + [swap(part, k << 1) for k in (1, 2, 3)])
    part = jnp.stack([part, swap(part, 1)])
    return part.reshape(CHUNKS, 8 * SUB, COLS)


def local(
    fields,
    target,
    wet_levels,
    tile_links,
    tile_owner,
    kernel,
    norm_gain,
    weight_in,
    weight_out,
    layer_scale,
):
    tile_at = lax.axis_index("tile").astype(jnp.int32)
    ens_at = lax.axis_index("ens").astype(jnp.int32)
    own_slot = tile_at.reshape(1)
    me = ((tile_at & 1) * 16 + ((tile_at >> 1) & 3) * 4 + (ens_at >> 1)).reshape(1)
    level_of = jnp.arange(TILES * PARTS, dtype=jnp.int32) * LEVELS // CH
    wet_mask = wet_levels[0][None, :, :] > level_of[:, None, None]
    own_input = jnp.pad(fields[0, 0], ((0, TILES * PARTS - CH), (0, 0), (0, 0)))
    payload = jnp.where(wet_mask, own_input, jnp.zeros_like(own_input))
    coef = jnp.concatenate([kernel, norm_gain[:, None], layer_scale[:, None]], axis=1)

    own_rows, wide, flat_masked = prepare(payload, coef)
    chunks = lax.all_to_all(
        payload.reshape(TILES, PARTS, ROWS, COLS), "tile", 0, 0, tiled=True
    )
    rims = lax.all_to_all(compose(tile_links, tile_owner, chunks), "tile", 0, 0, tiled=True)
    rims = rims.reshape(TILES * PARTS, ROWS, COLS)
    centred, flat_norm, inv_std, ext, halo = forward_conv(
        tile_links, tile_owner, own_slot, own_rows, wide, rims, coef
    )

    scale_wide = layer_scale[:, None]
    hidden = jnp.einsum("ch,cp->hp", weight_in, flat_norm, preferred_element_type=f32)
    activated = gelu_value(hidden).astype(bf16)
    mlp_out = jnp.einsum("hc,hp->cp", weight_out, activated, preferred_element_type=f32)
    block_out = (flat_masked.astype(f32) + scale_wide * mlp_out).astype(bf16)
    flat_wet = wet_levels[0].reshape(1, CELLS) > level_of[:CH, None]
    misfit = jnp.where(
        flat_wet, block_out.astype(f32) - target[0, 0].reshape(CH, CELLS).astype(f32), 0.0
    )
    grad_mlp = (2.0 * scale_wide * misfit).astype(bf16)
    part_out = jnp.einsum("cp,hp->ch", grad_mlp, activated, preferred_element_type=f32)
    grad_act = jnp.einsum("hc,cp->hp", weight_out, grad_mlp, preferred_element_type=f32)
    grad_hidden = (grad_act * gelu_slope(hidden)).astype(bf16)
    part_in = jnp.einsum("cp,hp->ch", flat_norm, grad_hidden, preferred_element_type=f32)
    grad_normed = jnp.einsum("ch,hp->cp", weight_in, grad_hidden, preferred_element_type=f32)

    packed = backward_conv(
        me, grad_normed, centred, inv_std, own_rows, ext, halo, coef, part_in, part_out
    )
    grad_in, grad_out, grad_taps = unpack(me, reduce_all(packed))
    return block_out.reshape(1, 1, CH, ROWS, COLS), grad_in, grad_out.T, grad_taps.T


def solution(mesh):
    placed = (
        P("ens", "tile", None, None, None),
        P("ens", "tile", None, None, None),
        P("tile", None, None),
        P(),
        P(),
        P(),
        P(),
        P(),
        P(),
        P(),
    )
    return jax.shard_map(
        local,
        mesh=mesh,
        in_specs=placed,
        out_specs=(P("ens", "tile", None, None, None), P(), P(), P()),
        check_vma=False,
    )
```

```python
import jax
import jax.numpy as jnp
from jax import lax
from jax.experimental import pallas as pl
from jax.experimental.pallas import tpu as pltpu
from jax.sharding import Mesh
from jax.sharding import PartitionSpec as P

LEVELS = 19
TILES = 32
CH = 200
PARTS = 7
ROWS = 8
COLS = 128
EXT = 14
TAPS = 7
HID = 800
CELLS = ROWS * COLS
CHUNKS = 32
SUB = 11
TILES_IN = 175

root_half = 0.7071067811865476
gauss_norm = 0.3989422804014327
norm_epsilon = 1e-06
f32 = jnp.float32
bf16 = jnp.bfloat16
TILE = ("zl", "x", "core")
BIG = 24 << 20


def gelu_value(values):
    return 0.5 * values * (1.0 + lax.erf(values * root_half))


def gelu_slope(values):
    return (
        0.5 * (1.0 + lax.erf(values * root_half))
        + values * jnp.exp(-0.5 * values * values) * gauss_norm
    )


def link_at(table, tile_id, column):
    return jnp.where(tile_id >= 0, table[jnp.maximum(tile_id, 0), column], -1)


def compose_kernel(table, x_ref, o_ref, inverse):
    shape = (PARTS, ROWS, COLS)
    row = lax.broadcasted_iota(jnp.int32, shape, 1)
    lane = lax.broadcasted_iota(jnp.int32, shape, 2)
    edge = (lane < 3) | (lane >= COLS - 3)
    east_side = lane < 64

    def note(k, _):
        inverse[table[k, 5]] = k
        return 0

    lax.fori_loop(0, TILES, note, 0)

    def load(tile_id):
        slot = jnp.maximum(link_at(table, tile_id, 5), 0)
        block = x_ref[slot].astype(f32)
        return jnp.where(tile_id >= 0, block, 0.0)

    def north_of(tile_id):
        block = load(link_at(table, tile_id, 0))
        return jnp.where(link_at(table, tile_id, 4) == 1, pltpu.roll(block, 3, 1), block)

    def body(d, _):
        own = inverse[d]
        west = link_at(table, own, 2)
        east = link_at(table, own, 3)
        north_rows = north_of(own)
        south_rows = load(link_at(table, own, 1))
        sides = jnp.where(edge, jnp.where(east_side, load(east), load(west)), 0.0)
        north_side = (lane < 64) != (link_at(table, own, 4) == 1)
        north_corner = jnp.where(north_side, north_of(east), north_of(west))
        south_corner = jnp.where(
            east_side, load(link_at(table, east, 1)), load(link_at(table, west, 1))
        )
        corners = jnp.where(row < 3, north_corner, south_corner)
        corners = jnp.where(edge & ((row < 3) | (row > 4)), corners, 0.0)
        spread = pltpu.roll(
            sides + pltpu.roll(corners, 64, 2), 24, 2, stride=8, stride_axis=1
        )
        packed = jnp.sum(spread, axis=1, keepdims=True)
        block = jnp.where(row == 3, packed, jnp.where(row < 3, north_rows, south_rows))
        o_ref[d] = block.astype(bf16)
        return 0

    lax.fori_loop(0, TILES, body, 0, unroll=8)


def compose(table, chunks):
    smem = pl.BlockSpec(memory_space=pltpu.SMEM)
    vmem = pl.BlockSpec(memory_space=pltpu.VMEM)
    return pl.pallas_call(
        compose_kernel,
        out_shape=jax.ShapeDtypeStruct((TILES, PARTS, ROWS, COLS), bf16),
        in_specs=[smem, vmem],
        out_specs=vmem,
        scratch_shapes=[pltpu.SMEM((TILES,), jnp.int32)],
        compiler_params=pltpu.CompilerParams(vmem_limit_bytes=BIG),
        name="compose",
    )(table, chunks)


def chosen(center, halo, col_off, lane):
    if col_off < 3:
        return jnp.where(lane >= COLS - 3 + col_off, halo, center)
    if col_off > 3:
        return jnp.where(lane < col_off - 3, halo, center)
    return center


def turned(values, col_off):
    return values if col_off == 3 else pltpu.roll(values, (3 - col_off) % COLS, 1)


def extended_rows(own_rows, ext, halo, at, col_off, lane):
    rows = [ext[r, at, :] for r in range(3)]
    rows += [own_rows[r, at, :] for r in range(ROWS)]
    rows += [ext[r, at, :] for r in range(3, 6)]
    return [chosen(x, halo[r, at, :], col_off, lane) for r, x in enumerate(rows)]


def prepare_kernel(table, own_slot, m_ref, coef, own, taps, flat_ref, turn_ref, fold_ref, mine, wide, sent):
    for k in range(TAPS * TAPS):
        wide[k] = jnp.broadcast_to(coef[:, k : k + 1], (CH, COLS))
    store = pltpu.make_async_copy(wide, taps, sent)
    store.start()
    mine[...] = m_ref[0:CH].astype(f32).reshape(CH * ROWS, COLS)
    for r in range(ROWS):
        values = mine[pl.ds(r, CH, stride=ROWS), :]
        own[r] = values
        flat_ref[:, COLS * r : COLS * r + COLS] = values.astype(bf16)
    slot = own_slot[0]

    def find(k, best):
        return jnp.where(table[k, 5] == slot, k, best)

    fold = table[lax.fori_loop(0, TILES, find, 0), 4] == 1
    row = lax.broadcasted_iota(jnp.int32, (COLS, COLS), 0)
    col = lax.broadcasted_iota(jnp.int32, (COLS, COLS), 1)
    turn_ref[...] = (row == jnp.where(fold, COLS - 1 - col, col)).astype(f32).astype(bf16)
    fold_ref[...] = jnp.broadcast_to(jnp.where(fold, 1, 0), (8, COLS))
    store.wait()


def prepare(table, own_slot, payload, coef):
    smem = pl.BlockSpec(memory_space=pltpu.SMEM)
    vmem = pl.BlockSpec(memory_space=pltpu.VMEM)
    wide = (TAPS * TAPS, CH, COLS)
    return pl.pallas_call(
        prepare_kernel,
        out_shape=[
            jax.ShapeDtypeStruct((ROWS, CH, COLS), f32),
            jax.ShapeDtypeStruct(wide, f32),
            jax.ShapeDtypeStruct((CH, CELLS), bf16),
            jax.ShapeDtypeStruct((COLS, COLS), bf16),
            jax.ShapeDtypeStruct((8, COLS), jnp.int32),
        ],
        in_specs=[smem, smem, vmem, vmem],
        out_specs=[vmem, pl.BlockSpec(memory_space=pltpu.HBM), vmem, vmem, vmem],
        scratch_shapes=[
            pltpu.VMEM((CH * ROWS, COLS), f32),
            pltpu.VMEM(wide, f32),
            pltpu.SemaphoreType.DMA,
        ],
        compiler_params=pltpu.CompilerParams(vmem_limit_bytes=BIG),
        name="prepare",
    )(table, own_slot, payload, coef)


def mask_kernel(fields, wet_levels, o_ref, held, wet_ref, arrived):
    cuts = (0, 56, 104, 152, CH)
    levels = pltpu.make_async_copy(wet_levels, wet_ref, arrived.at[4])
    levels.start()
    copies = []
    for n in range(4):
        span = pl.ds(cuts[n], cuts[n + 1] - cuts[n])
        copies.append(pltpu.make_async_copy(fields.at[span], held.at[span], arrived.at[n]))
        copies[n].start()
    levels.wait()
    wet = wet_ref[...].astype(f32) * CH
    for n in range(4):
        copies[n].wait()
        for c in range(cuts[n], cuts[n + 1]):
            value = held[c].astype(f32)
            o_ref[c] = jnp.where(wet > LEVELS * c, value, 0.0).astype(bf16)
    o_ref[CH:] = jnp.zeros((TILES * PARTS - CH, ROWS, COLS), bf16)


def mask_fields(fields, wet_levels):
    vmem = pl.BlockSpec(memory_space=pltpu.VMEM)
    return pl.pallas_call(
        mask_kernel,
        out_shape=jax.ShapeDtypeStruct((TILES * PARTS, ROWS, COLS), bf16),
        in_specs=[pl.BlockSpec(memory_space=pltpu.HBM)] * 2,
        out_specs=vmem,
        scratch_shapes=[
            pltpu.VMEM((CH, ROWS, COLS), bf16),
            pltpu.VMEM((ROWS, COLS), jnp.int32),
            pltpu.SemaphoreType.DMA((5,)),
        ],
        compiler_params=pltpu.CompilerParams(vmem_limit_bytes=BIG),
        name="mask_fields",
    )(*(pltpu.with_memory_space_constraint(x, pltpu.HBM) for x in (fields, wet_levels)))


def conv_kernel(
    own_rows, taps, r_ref, coef, turn_ref, fold_ref, cen_ref, norm_ref, inv_ref, ext, halo, rims, wide, arrived
):
    fetch = pltpu.make_async_copy(taps, wide, arrived)
    fetch.start()
    fold = jnp.broadcast_to(fold_ref[0:1, :], (CH, COLS)) == 1
    rims[...] = r_ref[0:CH].astype(f32).reshape(CH * ROWS, COLS)
    turn = turn_ref[...]
    edges = rims[pl.ds(3, CH, stride=ROWS), :]
    for r in range(11):
        halo[r] = edges if r == 0 else pltpu.roll(edges, COLS - 8 * r, 1)
    north = [rims[pl.ds(t, CH, stride=ROWS), :] for t in range(3)]
    corner = [pltpu.roll(edges, COLS - 8 * (11 + t), 1) for t in range(3)]
    for t in range(3):
        ext[t] = rims[pl.ds(5 + t, CH, stride=ROWS), :]
        for dest, source, first in ((ext, north, 3), (halo, corner, 11)):
            raw = jnp.where(fold, source[2 - t], source[t]).astype(bf16)
            dest[first + t] = jnp.dot(raw, turn, preferred_element_type=f32)
    lane = lax.broadcasted_iota(jnp.int32, (8, COLS), 1)
    fetch.wait()

    def block(i, sums):
        at = pl.ds(pl.multiple_of(8 * i, 8), 8)
        acc = [jnp.zeros((8, COLS), f32) for _ in range(ROWS)]
        for b in range(TAPS):
            moved = extended_rows(own_rows, ext, halo, at, b, lane)
            part = [None] * ROWS
            for a in range(TAPS):
                tap = wide[7 * a + b, at, :]
                for r in range(ROWS):
                    term = tap * moved[r + a]
                    part[r] = term if a == 0 else part[r] + term
            for r in range(ROWS):
                acc[r] = acc[r] + turned(part[r], b)
        for r in range(ROWS):
            cen_ref[at, COLS * r : COLS * r + COLS] = acc[r]
        return tuple(s + x for s, x in zip(sums, acc))

    sums = lax.fori_loop(0, CH // 8, block, tuple(jnp.zeros((8, COLS), f32) for _ in range(ROWS)))
    gain = jnp.broadcast_to(coef[:, 49:50], (CH, COLS))
    for r in range(ROWS):
        at = slice(COLS * r, COLS * r + COLS)
        mean = jnp.sum(sums[r], axis=0, keepdims=True) * (1.0 / CH)
        off = cen_ref[:, at] - mean
        var = jnp.sum(off * off, axis=0, keepdims=True) * (1.0 / CH)
        inv = 1.0 / jnp.sqrt(var + norm_epsilon)
        centred = off * inv
        cen_ref[:, at] = centred
        norm_ref[:, at] = (centred * gain).astype(bf16)
        inv_ref[r : r + 1, :] = inv


def forward_conv(own_rows, wide, rims, coef, turn, fold):
    vmem = pl.BlockSpec(memory_space=pltpu.VMEM)
    shapes = [
        ((CH, CELLS), f32),
        ((CH, CELLS), bf16),
        ((ROWS, COLS), f32),
        ((6, CH, COLS), f32),
        ((EXT, CH, COLS), f32),
    ]
    return pl.pallas_call(
        conv_kernel,
        out_shape=[jax.ShapeDtypeStruct(s, d) for s, d in shapes],
        in_specs=[vmem, pl.BlockSpec(memory_space=pltpu.HBM), vmem, vmem, vmem, vmem],
        out_specs=[vmem] * len(shapes),
        scratch_shapes=[
            pltpu.VMEM((CH * ROWS, COLS), f32),
            pltpu.VMEM((TAPS * TAPS, CH, COLS), f32),
            pltpu.SemaphoreType.DMA,
        ],
        compiler_params=pltpu.CompilerParams(vmem_limit_bytes=BIG),
        name="forward_conv",
    )(own_rows, pltpu.with_memory_space_constraint(wide, pltpu.HBM), rims, coef, turn, fold)


def grad_kernel(
    me, gn_ref, cen_ref, inv_ref, own_rows, ext, halo, coef, in_ref, out_ref, packed, gconv, terms_ref
):
    gain = jnp.broadcast_to(coef[:, 49:50], (CH, COLS))
    for r in range(ROWS):
        at = slice(COLS * r, COLS * r + COLS)
        scaled = gn_ref[:, at] * gain
        centred = cen_ref[:, at]
        mean = jnp.sum(scaled, axis=0, keepdims=True) * (1.0 / CH)
        along = jnp.sum(scaled * centred, axis=0, keepdims=True) * (1.0 / CH)
        gconv[:, at] = (scaled - mean - centred * along) * inv_ref[r : r + 1, :]
    lane = lax.broadcasted_iota(jnp.int32, (8, COLS), 1)

    def block(i, _):
        at = pl.ds(pl.multiple_of(8 * i, 8), 8)
        grads = [gconv[at, COLS * r : COLS * r + COLS] for r in range(ROWS)]
        for b in range(TAPS):
            moved = extended_rows(own_rows, ext, halo, at, b, lane)
            back = [turned(g, 6 - b) for g in grads]
            for a in range(TAPS):
                terms = back[0] * moved[a]
                for r in range(1, ROWS):
                    terms = terms + back[r] * moved[r + a]
                terms_ref[7 * a + b, at, :] = terms
        return 0

    lax.fori_loop(0, CH // 8, block, 0)
    ones = jnp.ones((COLS, COLS), bf16)
    wide_lane = lax.broadcasted_iota(jnp.int32, (CH, COLS), 1)
    found = jnp.zeros((CH, COLS), f32)
    for k in range(TAPS * TAPS):
        terms = terms_ref[k]
        high = terms.astype(bf16)
        low = (terms - high.astype(f32)).astype(bf16)
        total = jnp.dot(high, ones, preferred_element_type=f32)
        total = total + jnp.dot(low, ones, preferred_element_type=f32)
        found = jnp.where(wide_lane == 32 + k, total, found)
    place = [chunk ^ (16 * me[0]) for chunk in range(CHUNKS)]
    blank = jnp.zeros((8, 96), f32)
    for t in range(CHUNKS * SUB):
        source, at = (in_ref, t) if t < TILES_IN else (out_ref, t - TILES_IN)
        i, l = at // 7, at % 7
        if i >= CH // 8:
            tile = jnp.zeros((8, COLS), f32)
        elif l < 6:
            tile = source[8 * i : 8 * i + 8, COLS * l : COLS * l + COLS]
        else:
            tile = jnp.concatenate([source[8 * i : 8 * i + 8, 6 * COLS : HID], blank], axis=1)
            if t < TILES_IN:
                tile = jnp.where(lane < 32, tile, found[8 * i : 8 * i + 8, :])
        at = 8 * (t % SUB)
        packed[place[t // SUB], at : at + 8, :] = tile


def backward_conv(me, gn, cen, inv, own_rows, ext, halo, coef, part_in, part_out):
    smem = pl.BlockSpec(memory_space=pltpu.SMEM)
    vmem = pl.BlockSpec(memory_space=pltpu.VMEM)
    return pl.pallas_call(
        grad_kernel,
        out_shape=jax.ShapeDtypeStruct((CHUNKS, 8 * SUB, COLS), f32),
        in_specs=[smem] + [vmem] * 9,
        out_specs=vmem,
        scratch_shapes=[
            pltpu.VMEM((CH, CELLS), f32),
            pltpu.VMEM((TAPS * TAPS, CH, COLS), f32),
        ],
        compiler_params=pltpu.CompilerParams(vmem_limit_bytes=BIG),
        name="backward_conv",
    )(me, gn, cen, inv, own_rows, ext, halo, coef, part_in, part_out)


def unpack_kernel(me, own_half, other_half, in_ref, out_ref, k_ref, taps):
    share = 1.0 / (8 * TILES * CH * CELLS)
    for chunk in range(CHUNKS):
        mine = me[0] == chunk // 16
        values = jnp.where(mine, own_half[chunk % 16], other_half[chunk % 16]).astype(f32) * share
        for p in range(SUB):
            t = SUB * chunk + p
            dest, at = (in_ref, t) if t < TILES_IN else (out_ref, t - TILES_IN)
            i, l = at // 7, at % 7
            tile = values[8 * p : 8 * p + 8, :]
            if i >= CH // 8:
                continue
            if l < 6:
                dest[8 * i : 8 * i + 8, COLS * l : COLS * l + COLS] = tile
            else:
                dest[8 * i : 8 * i + 8, 6 * COLS : HID] = tile[:, 0:32]
                if t < TILES_IN:
                    taps[8 * i : 8 * i + 8, :] = tile
    taps[CH:256, :] = jnp.zeros((256 - CH, COLS), f32)
    k_ref[...] = jnp.transpose(taps[...])[32:81, 0:CH]


def unpack(me, own_half, other_half):
    vmem = pl.BlockSpec(memory_space=pltpu.VMEM)
    return pl.pallas_call(
        unpack_kernel,
        out_shape=[
            jax.ShapeDtypeStruct((CH, HID), f32),
            jax.ShapeDtypeStruct((CH, HID), f32),
            jax.ShapeDtypeStruct((49, CH), f32),
        ],
        in_specs=[pl.BlockSpec(memory_space=pltpu.SMEM), vmem, vmem],
        out_specs=[vmem] * 3,
        scratch_shapes=[pltpu.VMEM((256, COLS), f32)],
        compiler_params=pltpu.CompilerParams(vmem_limit_bytes=BIG),
        name="unpack",
    )(me, own_half, other_half)


def swap(values, axis, bits):
    size = lax.axis_size(axis)
    return lax.ppermute(values, axis, [(i, i ^ bits) for i in range(size)])


def reduce_all(held):
    held = held[:16] + swap(held[16:], "core", 1)
    parts = lax.all_to_all(held.astype(bf16), ("y", "x"), 0, 0, tiled=True)
    held = jnp.sum(parts.astype(f32), axis=0)
    held = (held + swap(held, "zl", 1)) + (swap(held, "zl", 2) + swap(held, "zl", 3))
    held = held + swap(held, "zh", 1)
    copies = jnp.broadcast_to(held.astype(bf16)[None], (16, 8 * SUB, COLS))
    half = lax.all_to_all(copies, ("y", "x"), 0, 0, tiled=True)
    return half, swap(half, "core", 1)


def local(
    fields,
    target,
    wet_levels,
    tile_links,
    tile_owner,
    kernel,
    norm_gain,
    weight_in,
    weight_out,
    layer_scale,
):
    own_slot = lax.axis_index(TILE).astype(jnp.int32).reshape(1)
    me = lax.axis_index("core").astype(jnp.int32).reshape(1)
    table = jnp.concatenate([tile_links, tile_owner[:, None]], axis=1)
    level_of = jnp.arange(CH, dtype=jnp.int32) * LEVELS // CH
    payload = mask_fields(fields[0, 0], wet_levels[0])
    coef = jnp.concatenate([kernel, norm_gain[:, None], layer_scale[:, None]], axis=1)

    own_rows, wide, flat_masked, turn, fold = prepare(table, own_slot, payload, coef)
    chunks = lax.all_to_all(payload.reshape(TILES, PARTS, ROWS, COLS), TILE, 0, 0, tiled=True)
    rims = lax.all_to_all(compose(table, chunks), TILE, 0, 0, tiled=True)
    rims = rims.reshape(TILES * PARTS, ROWS, COLS)
    centred, flat_norm, inv_std, ext, halo = forward_conv(own_rows, wide, rims, coef, turn, fold)

    scale_wide = layer_scale[:, None]
    hidden = jnp.einsum("ch,cp->hp", weight_in, flat_norm, preferred_element_type=f32)
    activated = gelu_value(hidden).astype(bf16)
    mlp_out = jnp.einsum("hc,hp->cp", weight_out, activated, preferred_element_type=f32)
    block_out = (flat_masked.astype(f32) + scale_wide * mlp_out).astype(bf16)
    flat_wet = wet_levels[0].reshape(1, CELLS) > level_of[:, None]
    misfit = jnp.where(
        flat_wet, block_out.astype(f32) - target[0, 0].reshape(CH, CELLS).astype(f32), 0.0
    )
    grad_mlp = (2.0 * scale_wide * misfit).astype(bf16)
    part_out = jnp.einsum("cp,hp->ch", grad_mlp, activated, preferred_element_type=f32)
    grad_act = jnp.einsum("hc,cp->hp", weight_out, grad_mlp, preferred_element_type=f32)
    grad_hidden = (grad_act * gelu_slope(hidden)).astype(bf16)
    part_in = jnp.einsum("cp,hp->ch", flat_norm, grad_hidden, preferred_element_type=f32)
    grad_normed = jnp.einsum("ch,hp->cp", weight_in, grad_hidden, preferred_element_type=f32)

    packed = backward_conv(
        me, grad_normed, centred, inv_std, own_rows, ext, halo, coef, part_in, part_out
    )
    grad_in, grad_out, grad_taps = unpack(me, *reduce_all(packed))
    return block_out.reshape(1, 1, CH, ROWS, COLS), grad_in, grad_out.T, grad_taps.T


def solution(mesh):
    fine = Mesh(mesh.devices.reshape(4, 2, 4, 4, 2), ("y", "zh", "zl", "x", "core"))
    big = P(("y", "zh"), TILE, None, None, None)
    placed = (big, big, P(TILE, None, None)) + (P(),) * 7
    return jax.shard_map(
        local,
        mesh=fine,
        in_specs=placed,
        out_specs=(big, P(), P(), P()),
        check_vma=False,
    )
```

```python
import jax
import jax.numpy as jnp
from jax import lax
from jax.experimental import pallas as pl
from jax.experimental.pallas import tpu as pltpu
from jax.sharding import Mesh
from jax.sharding import PartitionSpec as P

LEVELS = 19
TILES = 32
CH = 200
PARTS = 7
ROWS = 8
COLS = 128
EXT = 14
TAPS = 7
HID = 800
CELLS = ROWS * COLS
CHUNKS = 32
SUB = 11
TILES_IN = 175

root_half = 0.7071067811865476
gauss_norm = 0.3989422804014327
norm_epsilon = 1e-06
f32 = jnp.float32
bf16 = jnp.bfloat16
TILE = ("zl", "x", "core")
ROUTE = ("core", "x", "zl")
BIG = 24 << 20


def gelu_value(values):
    return 0.5 * values * (1.0 + lax.erf(values * root_half))


def gelu_slope(values):
    return (
        0.5 * (1.0 + lax.erf(values * root_half))
        + values * jnp.exp(-0.5 * values * values) * gauss_norm
    )


def link_at(table, tile_id, column):
    return jnp.where(tile_id >= 0, table[jnp.maximum(tile_id, 0), column], -1)


def compose_kernel(table, x_ref, o_ref, inverse):
    shape = (PARTS, ROWS, COLS)
    row = lax.broadcasted_iota(jnp.int32, shape, 1)
    lane = lax.broadcasted_iota(jnp.int32, shape, 2)
    edge = (lane < 3) | (lane >= COLS - 3)
    east_side = lane < 64

    def note(k, _):
        inverse[table[k, 5]] = k
        return 0

    lax.fori_loop(0, TILES, note, 0)

    def load(tile_id):
        slot = jnp.maximum(link_at(table, tile_id, 5), 0)
        block = x_ref[slot].astype(f32)
        return jnp.where(tile_id >= 0, block, 0.0)

    def north_of(tile_id):
        block = load(link_at(table, tile_id, 0))
        return jnp.where(link_at(table, tile_id, 4) == 1, pltpu.roll(block, 3, 1), block)

    def body(d, _):
        own = inverse[d]
        west = link_at(table, own, 2)
        east = link_at(table, own, 3)
        north_rows = north_of(own)
        south_rows = load(link_at(table, own, 1))
        sides = jnp.where(edge, jnp.where(east_side, load(east), load(west)), 0.0)
        north_side = (lane < 64) != (link_at(table, own, 4) == 1)
        north_corner = jnp.where(north_side, north_of(east), north_of(west))
        south_corner = jnp.where(
            east_side, load(link_at(table, east, 1)), load(link_at(table, west, 1))
        )
        corners = jnp.where(row < 3, north_corner, south_corner)
        corners = jnp.where(edge & ((row < 3) | (row > 4)), corners, 0.0)
        spread = pltpu.roll(
            sides + pltpu.roll(corners, 64, 2), 24, 2, stride=8, stride_axis=1
        )
        packed = jnp.sum(spread, axis=1, keepdims=True)
        block = jnp.where(row == 3, packed, jnp.where(row < 3, north_rows, south_rows))
        o_ref[d] = block.astype(bf16)
        return 0

    lax.fori_loop(0, TILES, body, 0, unroll=8)


def compose(table, chunks):
    smem = pl.BlockSpec(memory_space=pltpu.SMEM)
    vmem = pl.BlockSpec(memory_space=pltpu.VMEM)
    return pl.pallas_call(
        compose_kernel,
        out_shape=jax.ShapeDtypeStruct((TILES, PARTS, ROWS, COLS), bf16),
        in_specs=[smem, vmem],
        out_specs=vmem,
        scratch_shapes=[pltpu.SMEM((TILES,), jnp.int32)],
        compiler_params=pltpu.CompilerParams(vmem_limit_bytes=BIG),
        name="compose",
    )(table, chunks)


def chosen(center, halo, col_off, lane):
    if col_off < 3:
        return jnp.where(lane >= COLS - 3 + col_off, halo, center)
    if col_off > 3:
        return jnp.where(lane < col_off - 3, halo, center)
    return center


def turned(values, col_off):
    return values if col_off == 3 else pltpu.roll(values, (3 - col_off) % COLS, 1)


def extended_rows(own_rows, ext, halo, at, col_off, lane):
    rows = [ext[r, at, :] for r in range(3)]
    rows += [own_rows[r, at, :] for r in range(ROWS)]
    rows += [ext[r, at, :] for r in range(3, 6)]
    return [chosen(x, halo[r, at, :], col_off, lane) for r, x in enumerate(rows)]


def prepare_kernel(table, own_slot, m_ref, coef, own, taps, flat_ref, turn_ref, fold_ref, mine, wide, sent):
    for k in range(TAPS * TAPS):
        wide[k] = jnp.broadcast_to(coef[:, k : k + 1], (CH, COLS))
    store = pltpu.make_async_copy(wide, taps, sent)
    store.start()
    mine[...] = m_ref[0:CH].astype(f32).reshape(CH * ROWS, COLS)
    for r in range(ROWS):
        values = mine[pl.ds(r, CH, stride=ROWS), :]
        own[r] = values
        flat_ref[:, COLS * r : COLS * r + COLS] = values.astype(bf16)
    slot = own_slot[0]

    def find(k, best):
        return jnp.where(table[k, 5] == slot, k, best)

    fold = table[lax.fori_loop(0, TILES, find, 0), 4] == 1
    row = lax.broadcasted_iota(jnp.int32, (COLS, COLS), 0)
    col = lax.broadcasted_iota(jnp.int32, (COLS, COLS), 1)
    turn_ref[...] = (row == jnp.where(fold, COLS - 1 - col, col)).astype(f32).astype(bf16)
    fold_ref[...] = jnp.broadcast_to(jnp.where(fold, 1, 0), (8, COLS))
    store.wait()


def prepare(table, own_slot, payload, coef):
    smem = pl.BlockSpec(memory_space=pltpu.SMEM)
    vmem = pl.BlockSpec(memory_space=pltpu.VMEM)
    wide = (TAPS * TAPS, CH, COLS)
    return pl.pallas_call(
        prepare_kernel,
        out_shape=[
            jax.ShapeDtypeStruct((ROWS, CH, COLS), f32),
            jax.ShapeDtypeStruct(wide, f32),
            jax.ShapeDtypeStruct((CH, CELLS), bf16),
            jax.ShapeDtypeStruct((COLS, COLS), bf16),
            jax.ShapeDtypeStruct((8, COLS), jnp.int32),
        ],
        in_specs=[smem, smem, vmem, vmem],
        out_specs=[vmem, pl.BlockSpec(memory_space=pltpu.HBM), vmem, vmem, vmem],
        scratch_shapes=[
            pltpu.VMEM((CH * ROWS, COLS), f32),
            pltpu.VMEM(wide, f32),
            pltpu.SemaphoreType.DMA,
        ],
        compiler_params=pltpu.CompilerParams(vmem_limit_bytes=BIG),
        name="prepare",
    )(table, own_slot, payload, coef)


def mask_kernel(fields, wet_levels, o_ref, held, wet_ref, arrived):
    cuts = (0, 56, 104, 152, CH)
    levels = pltpu.make_async_copy(wet_levels, wet_ref, arrived.at[4])
    levels.start()
    copies = []
    for n in range(4):
        span = pl.ds(cuts[n], cuts[n + 1] - cuts[n])
        copies.append(pltpu.make_async_copy(fields.at[span], held.at[span], arrived.at[n]))
        copies[n].start()
    levels.wait()
    wet = wet_ref[...].astype(f32).astype(bf16)
    dry = jnp.zeros((ROWS, COLS), bf16)
    for n in range(4):
        copies[n].wait()
        for c in range(cuts[n], cuts[n + 1]):
            o_ref[c] = jnp.where(wet > bf16(LEVELS * c // CH), held[c], dry)
    o_ref[CH:] = jnp.zeros((TILES * PARTS - CH, ROWS, COLS), bf16)


def mask_fields(fields, wet_levels):
    vmem = pl.BlockSpec(memory_space=pltpu.VMEM)
    return pl.pallas_call(
        mask_kernel,
        out_shape=jax.ShapeDtypeStruct((TILES * PARTS, ROWS, COLS), bf16),
        in_specs=[pl.BlockSpec(memory_space=pltpu.HBM)] * 2,
        out_specs=vmem,
        scratch_shapes=[
            pltpu.VMEM((CH, ROWS, COLS), bf16),
            pltpu.VMEM((ROWS, COLS), jnp.int32),
            pltpu.SemaphoreType.DMA((5,)),
        ],
        compiler_params=pltpu.CompilerParams(vmem_limit_bytes=BIG),
        name="mask_fields",
    )(*(pltpu.with_memory_space_constraint(x, pltpu.HBM) for x in (fields, wet_levels)))


def conv_kernel(
    own_rows, taps, r_ref, coef, turn_ref, fold_ref, cen_ref, norm_ref, inv_ref, ext, halo, rims, wide, arrived
):
    fetch = pltpu.make_async_copy(taps, wide, arrived)
    fetch.start()
    fold = jnp.broadcast_to(fold_ref[0:1, :], (CH, COLS)) == 1
    rims[...] = r_ref[0:CH].astype(f32).reshape(CH * ROWS, COLS)
    turn = turn_ref[...]
    edges = rims[pl.ds(3, CH, stride=ROWS), :]
    for r in range(11):
        halo[r] = edges if r == 0 else pltpu.roll(edges, COLS - 8 * r, 1)
    north = [rims[pl.ds(t, CH, stride=ROWS), :] for t in range(3)]
    corner = [pltpu.roll(edges, COLS - 8 * (11 + t), 1) for t in range(3)]
    for t in range(3):
        ext[t] = rims[pl.ds(5 + t, CH, stride=ROWS), :]
        for dest, source, first in ((ext, north, 3), (halo, corner, 11)):
            raw = jnp.where(fold, source[2 - t], source[t]).astype(bf16)
            dest[first + t] = jnp.dot(raw, turn, preferred_element_type=f32)
    lane = lax.broadcasted_iota(jnp.int32, (8, COLS), 1)
    fetch.wait()

    def block(i, sums):
        at = pl.ds(pl.multiple_of(8 * i, 8), 8)
        acc = [jnp.zeros((8, COLS), f32) for _ in range(ROWS)]
        for b in range(TAPS):
            moved = extended_rows(own_rows, ext, halo, at, b, lane)
            part = [None] * ROWS
            for a in range(TAPS):
                tap = wide[7 * a + b, at, :]
                for r in range(ROWS):
                    term = tap * moved[r + a]
                    part[r] = term if a == 0 else part[r] + term
            for r in range(ROWS):
                acc[r] = acc[r] + turned(part[r], b)
        for r in range(ROWS):
            cen_ref[at, COLS * r : COLS * r + COLS] = acc[r]
        return tuple(s + x for s, x in zip(sums, acc))

    sums = lax.fori_loop(0, CH // 8, block, tuple(jnp.zeros((8, COLS), f32) for _ in range(ROWS)))
    gain = jnp.broadcast_to(coef[:, 49:50], (CH, COLS))
    for r in range(ROWS):
        at = slice(COLS * r, COLS * r + COLS)
        mean = jnp.sum(sums[r], axis=0, keepdims=True) * (1.0 / CH)
        off = cen_ref[:, at] - mean
        var = jnp.sum(off * off, axis=0, keepdims=True) * (1.0 / CH)
        inv = 1.0 / jnp.sqrt(var + norm_epsilon)
        centred = off * inv
        cen_ref[:, at] = centred
        norm_ref[:, at] = (centred * gain).astype(bf16)
        inv_ref[r : r + 1, :] = inv


def forward_conv(own_rows, wide, rims, coef, turn, fold):
    vmem = pl.BlockSpec(memory_space=pltpu.VMEM)
    shapes = [
        ((CH, CELLS), f32),
        ((CH, CELLS), bf16),
        ((ROWS, COLS), f32),
        ((6, CH, COLS), f32),
        ((EXT, CH, COLS), f32),
    ]
    return pl.pallas_call(
        conv_kernel,
        out_shape=[jax.ShapeDtypeStruct(s, d) for s, d in shapes],
        in_specs=[vmem, pl.BlockSpec(memory_space=pltpu.HBM), vmem, vmem, vmem, vmem],
        out_specs=[vmem] * len(shapes),
        scratch_shapes=[
            pltpu.VMEM((CH * ROWS, COLS), f32),
            pltpu.VMEM((TAPS * TAPS, CH, COLS), f32),
            pltpu.SemaphoreType.DMA,
        ],
        compiler_params=pltpu.CompilerParams(vmem_limit_bytes=BIG),
        name="forward_conv",
    )(own_rows, pltpu.with_memory_space_constraint(wide, pltpu.HBM), rims, coef, turn, fold)


def grad_kernel(
    me, gn_ref, cen_ref, inv_ref, own_rows, ext, halo, coef, in_ref, out_ref, keep, send, gconv, terms_ref
):
    gain = jnp.broadcast_to(coef[:, 49:50], (CH, COLS))
    for r in range(ROWS):
        at = slice(COLS * r, COLS * r + COLS)
        scaled = gn_ref[:, at] * gain
        centred = cen_ref[:, at]
        mean = jnp.sum(scaled, axis=0, keepdims=True) * (1.0 / CH)
        along = jnp.sum(scaled * centred, axis=0, keepdims=True) * (1.0 / CH)
        gconv[:, at] = (scaled - mean - centred * along) * inv_ref[r : r + 1, :]
    lane = lax.broadcasted_iota(jnp.int32, (8, COLS), 1)

    def block(i, _):
        at = pl.ds(pl.multiple_of(8 * i, 8), 8)
        grads = [gconv[at, COLS * r : COLS * r + COLS] for r in range(ROWS)]
        for b in range(TAPS):
            moved = extended_rows(own_rows, ext, halo, at, b, lane)
            back = [turned(g, 6 - b) for g in grads]
            for a in range(TAPS):
                terms = back[0] * moved[a]
                for r in range(1, ROWS):
                    terms = terms + back[r] * moved[r + a]
                terms_ref[7 * a + b, at, :] = terms
        return 0

    lax.fori_loop(0, CH // 8, block, 0)
    ones = jnp.ones((2 * COLS, COLS), bf16)
    wide_lane = lax.broadcasted_iota(jnp.int32, (CH, COLS), 1)
    found = jnp.zeros((CH, COLS), f32)
    for k in range(TAPS * TAPS):
        terms = terms_ref[k]
        high = terms.astype(bf16)
        low = (terms - high.astype(f32)).astype(bf16)
        both = jnp.concatenate([high, low], axis=1)
        total = jnp.dot(both, ones, preferred_element_type=f32)
        found = jnp.where(wide_lane == 32 + k, total, found)
    blank = jnp.zeros((8, 96), f32)

    def pack(halves):
        for t in range(CHUNKS * SUB):
            source, at = (in_ref, t) if t < TILES_IN else (out_ref, t - TILES_IN)
            i, l = at // 7, at % 7
            if i >= CH // 8:
                tile = jnp.zeros((8, COLS), f32)
            elif l < 6:
                tile = source[8 * i : 8 * i + 8, COLS * l : COLS * l + COLS]
            else:
                tile = jnp.concatenate([source[8 * i : 8 * i + 8, 6 * COLS : HID], blank], axis=1)
                if t < TILES_IN:
                    tile = jnp.where(lane < 32, tile, found[8 * i : 8 * i + 8, :])
            chunk, at = t // SUB, 8 * (t % SUB)
            halves[chunk // 16][chunk % 16, at : at + 8, :] = tile

    pl.when(me[0] == 0)(lambda: pack((keep, send)))
    pl.when(me[0] == 1)(lambda: pack((send, keep)))


def backward_conv(me, gn, cen, inv, own_rows, ext, halo, coef, part_in, part_out):
    smem = pl.BlockSpec(memory_space=pltpu.SMEM)
    vmem = pl.BlockSpec(memory_space=pltpu.VMEM)
    return pl.pallas_call(
        grad_kernel,
        out_shape=[jax.ShapeDtypeStruct((CHUNKS // 2, 8 * SUB, COLS), f32)] * 2,
        in_specs=[smem] + [vmem] * 9,
        out_specs=[vmem] * 2,
        scratch_shapes=[
            pltpu.VMEM((CH, CELLS), f32),
            pltpu.VMEM((TAPS * TAPS, CH, COLS), f32),
        ],
        compiler_params=pltpu.CompilerParams(vmem_limit_bytes=BIG),
        name="backward_conv",
    )(me, gn, cen, inv, own_rows, ext, halo, coef, part_in, part_out)


def unpack_kernel(me, own_half, other_half, in_ref, out_ref, k_ref, taps):
    share = 1.0 / (8 * TILES * CH * CELLS)

    def spread(halves):
        for chunk in range(CHUNKS):
            values = halves[chunk // 16][chunk % 16].astype(f32) * share
            for p in range(SUB):
                t = SUB * chunk + p
                dest, at = (in_ref, t) if t < TILES_IN else (out_ref, t - TILES_IN)
                i, l = at // 7, at % 7
                tile = values[8 * p : 8 * p + 8, :]
                if i >= CH // 8:
                    continue
                if l < 6:
                    dest[8 * i : 8 * i + 8, COLS * l : COLS * l + COLS] = tile
                else:
                    dest[8 * i : 8 * i + 8, 6 * COLS : HID] = tile[:, 0:32]
                    if t < TILES_IN:
                        taps[8 * i : 8 * i + 8, :] = tile

    pl.when(me[0] == 0)(lambda: spread((own_half, other_half)))
    pl.when(me[0] == 1)(lambda: spread((other_half, own_half)))
    taps[CH:256, :] = jnp.zeros((256 - CH, COLS), f32)
    k_ref[...] = jnp.transpose(taps[...])[32:81, 0:CH]


def unpack(me, own_half, other_half):
    vmem = pl.BlockSpec(memory_space=pltpu.VMEM)
    return pl.pallas_call(
        unpack_kernel,
        out_shape=[
            jax.ShapeDtypeStruct((CH, HID), f32),
            jax.ShapeDtypeStruct((CH, HID), f32),
            jax.ShapeDtypeStruct((49, CH), f32),
        ],
        in_specs=[pl.BlockSpec(memory_space=pltpu.SMEM), vmem, vmem],
        out_specs=[vmem] * 3,
        scratch_shapes=[pltpu.VMEM((256, COLS), f32)],
        compiler_params=pltpu.CompilerParams(vmem_limit_bytes=BIG),
        name="unpack",
    )(me, own_half, other_half)


def swap(values, axis, bits):
    size = lax.axis_size(axis)
    return lax.ppermute(values, axis, [(i, i ^ bits) for i in range(size)])


def reduce_all(keep, send):
    held = keep + swap(send, "core", 1)
    parts = lax.all_to_all(held.astype(bf16), ("x", "y"), 0, 0, tiled=True)
    held = jnp.sum(parts.astype(f32), axis=0)
    held = (held + swap(held, "zl", 1)) + (swap(held, "zl", 2) + swap(held, "zl", 3))
    held = held + swap(held, "zh", 1)
    copies = jnp.broadcast_to(held.astype(bf16)[None], (16, 8 * SUB, COLS))
    half = lax.all_to_all(copies, ("x", "y"), 0, 0, tiled=True)
    return half, swap(half, "core", 1)


def local(
    fields,
    target,
    wet_levels,
    tile_links,
    tile_owner,
    kernel,
    norm_gain,
    weight_in,
    weight_out,
    layer_scale,
):
    own_slot = lax.axis_index(ROUTE).astype(jnp.int32).reshape(1)
    me = lax.axis_index("core").astype(jnp.int32).reshape(1)
    place = (tile_owner & 1) * 16 + ((tile_owner >> 1) & 3) * 4 + (tile_owner >> 3)
    table = jnp.concatenate([tile_links, place[:, None]], axis=1)
    level_of = jnp.arange(CH, dtype=jnp.int32) * LEVELS // CH
    payload = mask_fields(fields[0, 0], wet_levels[0])
    coef = jnp.concatenate([kernel, norm_gain[:, None], layer_scale[:, None]], axis=1)

    own_rows, wide, flat_masked, turn, fold = prepare(table, own_slot, payload, coef)
    chunks = lax.all_to_all(payload.reshape(TILES, PARTS, ROWS, COLS), ROUTE, 0, 0, tiled=True)
    rims = lax.all_to_all(compose(table, chunks), ROUTE, 0, 0, tiled=True)
    rims = rims.reshape(TILES * PARTS, ROWS, COLS)
    centred, flat_norm, inv_std, ext, halo = forward_conv(own_rows, wide, rims, coef, turn, fold)

    scale_wide = layer_scale[:, None]
    hidden = jnp.einsum("ch,cp->hp", weight_in, flat_norm, preferred_element_type=f32)
    activated = gelu_value(hidden).astype(bf16)
    mlp_out = jnp.einsum("hc,hp->cp", weight_out, activated, preferred_element_type=f32)
    block_out = (flat_masked.astype(f32) + scale_wide * mlp_out).astype(bf16)
    flat_wet = wet_levels[0].reshape(1, CELLS) > level_of[:, None]
    misfit = jnp.where(
        flat_wet, block_out.astype(f32) - target[0, 0].reshape(CH, CELLS).astype(f32), 0.0
    )
    grad_mlp = (2.0 * scale_wide * misfit).astype(bf16)
    part_out = jnp.einsum("cp,hp->ch", grad_mlp, activated, preferred_element_type=f32)
    grad_act = jnp.einsum("hc,cp->hp", weight_out, grad_mlp, preferred_element_type=f32)
    grad_hidden = (grad_act * gelu_slope(hidden)).astype(bf16)
    part_in = jnp.einsum("cp,hp->ch", flat_norm, grad_hidden, preferred_element_type=f32)
    grad_normed = jnp.einsum("ch,hp->cp", weight_in, grad_hidden, preferred_element_type=f32)

    keep, send = backward_conv(
        me, grad_normed, centred, inv_std, own_rows, ext, halo, coef, part_in, part_out
    )
    grad_in, grad_out, grad_taps = unpack(me, *reduce_all(keep, send))
    return block_out.reshape(1, 1, CH, ROWS, COLS), grad_in, grad_out.T, grad_taps.T


def solution(mesh):
    fine = Mesh(mesh.devices.reshape(4, 2, 4, 4, 2), ("y", "zh", "zl", "x", "core"))
    big = P(("y", "zh"), TILE, None, None, None)
    placed = (big, big, P(TILE, None, None)) + (P(),) * 7
    return jax.shard_map(
        local,
        mesh=fine,
        in_specs=placed,
        out_specs=(big, P(), P(), P()),
        check_vma=False,
    )
```

```python
import jax
import jax.numpy as jnp
from jax import lax
from jax.experimental import pallas as pl
from jax.experimental.pallas import tpu as pltpu
from jax.sharding import Mesh
from jax.sharding import PartitionSpec as P

LEVELS = 19
TILES = 32
CH = 200
PARTS = 7
ROWS = 8
COLS = 128
EXT = 14
TAPS = 7
HID = 800
CELLS = ROWS * COLS
CHUNKS = 32
SUB = 11
TILES_IN = 175

root_half = 0.7071067811865476
gauss_norm = 0.3989422804014327
norm_epsilon = 1e-06
f32 = jnp.float32
bf16 = jnp.bfloat16
TILE = ("zl", "x", "core")
ROUTE = ("core", "x", "zl")
BIG = 24 << 20


def gelu_value(values):
    return 0.5 * values * (1.0 + lax.erf(values * root_half))


def gelu_slope(values):
    return (
        0.5 * (1.0 + lax.erf(values * root_half))
        + values * jnp.exp(-0.5 * values * values) * gauss_norm
    )


def link_at(table, tile_id, column):
    return jnp.where(tile_id >= 0, table[jnp.maximum(tile_id, 0), column], -1)


def compose_kernel(table, x_ref, o_ref, inverse):
    shape = (PARTS, ROWS, COLS)
    row = lax.broadcasted_iota(jnp.int32, shape, 1)
    lane = lax.broadcasted_iota(jnp.int32, shape, 2)
    edge = (lane < 3) | (lane >= COLS - 3)
    east_side = lane < 64

    def note(k, _):
        inverse[table[k, 5]] = k
        return 0

    lax.fori_loop(0, TILES, note, 0)

    def load(tile_id):
        slot = jnp.maximum(link_at(table, tile_id, 5), 0)
        block = x_ref[slot].astype(f32)
        return jnp.where(tile_id >= 0, block, 0.0)

    def north_of(tile_id):
        block = load(link_at(table, tile_id, 0))
        return jnp.where(link_at(table, tile_id, 4) == 1, pltpu.roll(block, 3, 1), block)

    def body(d, _):
        own = inverse[d]
        west = link_at(table, own, 2)
        east = link_at(table, own, 3)
        north_rows = north_of(own)
        south_rows = load(link_at(table, own, 1))
        sides = jnp.where(edge, jnp.where(east_side, load(east), load(west)), 0.0)
        north_side = (lane < 64) != (link_at(table, own, 4) == 1)
        north_corner = jnp.where(north_side, north_of(east), north_of(west))
        south_corner = jnp.where(
            east_side, load(link_at(table, east, 1)), load(link_at(table, west, 1))
        )
        corners = jnp.where(row < 3, north_corner, south_corner)
        corners = jnp.where(edge & ((row < 3) | (row > 4)), corners, 0.0)
        spread = pltpu.roll(
            sides + pltpu.roll(corners, 64, 2), 24, 2, stride=8, stride_axis=1
        )
        packed = jnp.sum(spread, axis=1, keepdims=True)
        block = jnp.where(row == 3, packed, jnp.where(row < 3, north_rows, south_rows))
        o_ref[d] = block.astype(bf16)
        return 0

    lax.fori_loop(0, TILES, body, 0, unroll=8)


def compose(table, chunks):
    smem = pl.BlockSpec(memory_space=pltpu.SMEM)
    vmem = pl.BlockSpec(memory_space=pltpu.VMEM)
    return pl.pallas_call(
        compose_kernel,
        out_shape=jax.ShapeDtypeStruct((TILES, PARTS, ROWS, COLS), bf16),
        in_specs=[smem, vmem],
        out_specs=vmem,
        scratch_shapes=[pltpu.SMEM((TILES,), jnp.int32)],
        compiler_params=pltpu.CompilerParams(vmem_limit_bytes=BIG),
        name="compose",
    )(table, chunks)


def chosen(center, halo, col_off, lane):
    if col_off < 3:
        return jnp.where(lane >= COLS - 3 + col_off, halo, center)
    if col_off > 3:
        return jnp.where(lane < col_off - 3, halo, center)
    return center


def turned(values, col_off):
    return values if col_off == 3 else pltpu.roll(values, (3 - col_off) % COLS, 1)


def extended_rows(own_rows, ext, halo, at, col_off, lane):
    rows = [ext[r, at, :] for r in range(3)]
    rows += [own_rows[r, at, :] for r in range(ROWS)]
    rows += [ext[r, at, :] for r in range(3, 6)]
    return [chosen(x, halo[r, at, :], col_off, lane) for r, x in enumerate(rows)]


def prepare_kernel(table, own_slot, m_ref, coef, own, taps, flat_ref, turn_ref, fold_ref, mine, wide, sent):

    def widen(i, _):
        taps_of = coef[pl.ds(pl.multiple_of(8 * i, 8), 8), :]
        for k in range(TAPS * TAPS):
            wide[i, k] = jnp.broadcast_to(taps_of[:, k : k + 1], (8, COLS))
        return 0

    lax.fori_loop(0, CH // 8, widen, 0, unroll=5)
    store = pltpu.make_async_copy(wide, taps, sent)
    store.start()
    mine[...] = m_ref[0:CH].astype(f32).reshape(CH * ROWS, COLS)
    for r in range(ROWS):
        values = mine[pl.ds(r, CH, stride=ROWS), :]
        own[r] = values
        flat_ref[:, COLS * r : COLS * r + COLS] = values.astype(bf16)
    slot = own_slot[0]

    def find(k, best):
        return jnp.where(table[k, 5] == slot, k, best)

    fold = table[lax.fori_loop(0, TILES, find, 0), 4] == 1
    row = lax.broadcasted_iota(jnp.int32, (COLS, COLS), 0)
    col = lax.broadcasted_iota(jnp.int32, (COLS, COLS), 1)
    turn_ref[...] = (row == jnp.where(fold, COLS - 1 - col, col)).astype(f32).astype(bf16)
    fold_ref[...] = jnp.broadcast_to(jnp.where(fold, 1, 0), (8, COLS))
    store.wait()


def prepare(table, own_slot, payload, coef):
    smem = pl.BlockSpec(memory_space=pltpu.SMEM)
    vmem = pl.BlockSpec(memory_space=pltpu.VMEM)
    wide = (CH // 8, TAPS * TAPS, 8, COLS)
    return pl.pallas_call(
        prepare_kernel,
        out_shape=[
            jax.ShapeDtypeStruct((ROWS, CH, COLS), f32),
            jax.ShapeDtypeStruct(wide, f32),
            jax.ShapeDtypeStruct((CH, CELLS), bf16),
            jax.ShapeDtypeStruct((COLS, COLS), bf16),
            jax.ShapeDtypeStruct((8, COLS), jnp.int32),
        ],
        in_specs=[smem, smem, vmem, vmem],
        out_specs=[vmem, pl.BlockSpec(memory_space=pltpu.HBM), vmem, vmem, vmem],
        scratch_shapes=[
            pltpu.VMEM((CH * ROWS, COLS), f32),
            pltpu.VMEM(wide, f32),
            pltpu.SemaphoreType.DMA,
        ],
        compiler_params=pltpu.CompilerParams(vmem_limit_bytes=BIG),
        name="prepare",
    )(table, own_slot, payload, coef)


def mask_kernel(fields, wet_levels, o_ref, held, wet_ref, arrived):
    cuts = (0, 56, 104, 152, CH)
    levels = pltpu.make_async_copy(wet_levels, wet_ref, arrived.at[4])
    levels.start()
    copies = []
    for n in range(4):
        span = pl.ds(cuts[n], cuts[n + 1] - cuts[n])
        copies.append(pltpu.make_async_copy(fields.at[span], held.at[span], arrived.at[n]))
        copies[n].start()
    levels.wait()
    wet = wet_ref[...].astype(f32).astype(bf16)
    dry = jnp.zeros((ROWS, COLS), bf16)
    for n in range(4):
        copies[n].wait()
        for c in range(cuts[n], cuts[n + 1]):
            o_ref[c] = jnp.where(wet > bf16(LEVELS * c // CH), held[c], dry)
    o_ref[CH:] = jnp.zeros((TILES * PARTS - CH, ROWS, COLS), bf16)


def mask_fields(fields, wet_levels):
    vmem = pl.BlockSpec(memory_space=pltpu.VMEM)
    return pl.pallas_call(
        mask_kernel,
        out_shape=jax.ShapeDtypeStruct((TILES * PARTS, ROWS, COLS), bf16),
        in_specs=[pl.BlockSpec(memory_space=pltpu.HBM)] * 2,
        out_specs=vmem,
        scratch_shapes=[
            pltpu.VMEM((CH, ROWS, COLS), bf16),
            pltpu.VMEM((ROWS, COLS), jnp.int32),
            pltpu.SemaphoreType.DMA((5,)),
        ],
        compiler_params=pltpu.CompilerParams(vmem_limit_bytes=BIG),
        name="mask_fields",
    )(*(pltpu.with_memory_space_constraint(x, pltpu.HBM) for x in (fields, wet_levels)))


def conv_kernel(
    own_rows, taps, r_ref, coef, turn_ref, fold_ref, cen_ref, norm_ref, inv_ref, ext, halo, rims, wide, arrived
):
    fetches = []
    for p in range(5):
        span = pl.ds(5 * p, 5)
        fetches.append(pltpu.make_async_copy(taps.at[span], wide.at[span], arrived.at[p]))
        fetches[p].start()
    fold = jnp.broadcast_to(fold_ref[0:1, :], (CH, COLS)) == 1
    rims[...] = r_ref[0:CH].astype(f32).reshape(CH * ROWS, COLS)
    turn = turn_ref[...]
    edges = rims[pl.ds(3, CH, stride=ROWS), :]
    for r in range(11):
        halo[r] = edges if r == 0 else pltpu.roll(edges, COLS - 8 * r, 1)
    north = [rims[pl.ds(t, CH, stride=ROWS), :] for t in range(3)]
    corner = [pltpu.roll(edges, COLS - 8 * (11 + t), 1) for t in range(3)]
    for t in range(3):
        ext[t] = rims[pl.ds(5 + t, CH, stride=ROWS), :]
        for dest, source, first in ((ext, north, 3), (halo, corner, 11)):
            raw = jnp.where(fold, source[2 - t], source[t]).astype(bf16)
            dest[first + t] = jnp.dot(raw, turn, preferred_element_type=f32)
    lane = lax.broadcasted_iota(jnp.int32, (8, COLS), 1)

    def block(i, sums):
        at = pl.ds(pl.multiple_of(8 * i, 8), 8)
        acc = [jnp.zeros((8, COLS), f32) for _ in range(ROWS)]
        for b in range(TAPS):
            moved = extended_rows(own_rows, ext, halo, at, b, lane)
            part = [None] * ROWS
            for a in range(TAPS):
                tap = wide[i, 7 * a + b]
                for r in range(ROWS):
                    term = tap * moved[r + a]
                    part[r] = term if a == 0 else part[r] + term
            for r in range(ROWS):
                acc[r] = acc[r] + turned(part[r], b)
        for r in range(ROWS):
            cen_ref[at, COLS * r : COLS * r + COLS] = acc[r]
        return tuple(s + x for s, x in zip(sums, acc))

    sums = tuple(jnp.zeros((8, COLS), f32) for _ in range(ROWS))
    for p in range(5):
        fetches[p].wait()
        sums = lax.fori_loop(5 * p, 5 * p + 5, block, sums)
    gain = jnp.broadcast_to(coef[:, 49:50], (CH, COLS))
    for r in range(ROWS):
        at = slice(COLS * r, COLS * r + COLS)
        mean = jnp.sum(sums[r], axis=0, keepdims=True) * (1.0 / CH)
        off = cen_ref[:, at] - mean
        var = jnp.sum(off * off, axis=0, keepdims=True) * (1.0 / CH)
        inv = 1.0 / jnp.sqrt(var + norm_epsilon)
        centred = off * inv
        cen_ref[:, at] = centred
        norm_ref[:, at] = (centred * gain).astype(bf16)
        inv_ref[r : r + 1, :] = inv


def forward_conv(own_rows, wide, rims, coef, turn, fold):
    vmem = pl.BlockSpec(memory_space=pltpu.VMEM)
    shapes = [
        ((CH, CELLS), f32),
        ((CH, CELLS), bf16),
        ((ROWS, COLS), f32),
        ((6, CH, COLS), f32),
        ((EXT, CH, COLS), f32),
    ]
    return pl.pallas_call(
        conv_kernel,
        out_shape=[jax.ShapeDtypeStruct(s, d) for s, d in shapes],
        in_specs=[vmem, pl.BlockSpec(memory_space=pltpu.HBM), vmem, vmem, vmem, vmem],
        out_specs=[vmem] * len(shapes),
        scratch_shapes=[
            pltpu.VMEM((CH * ROWS, COLS), f32),
            pltpu.VMEM((CH // 8, TAPS * TAPS, 8, COLS), f32),
            pltpu.SemaphoreType.DMA((5,)),
        ],
        compiler_params=pltpu.CompilerParams(vmem_limit_bytes=BIG),
        name="forward_conv",
    )(own_rows, pltpu.with_memory_space_constraint(wide, pltpu.HBM), rims, coef, turn, fold)


def grad_kernel(
    me, gn_ref, cen_ref, inv_ref, own_rows, ext, halo, coef, in_ref, out_ref, keep, send, gconv, terms_ref
):
    gain = jnp.broadcast_to(coef[:, 49:50], (CH, COLS))
    for r in range(ROWS):
        at = slice(COLS * r, COLS * r + COLS)
        scaled = gn_ref[:, at] * gain
        centred = cen_ref[:, at]
        mean = jnp.sum(scaled, axis=0, keepdims=True) * (1.0 / CH)
        along = jnp.sum(scaled * centred, axis=0, keepdims=True) * (1.0 / CH)
        gconv[:, at] = (scaled - mean - centred * along) * inv_ref[r : r + 1, :]
    lane = lax.broadcasted_iota(jnp.int32, (8, COLS), 1)

    def block(i, _):
        at = pl.ds(pl.multiple_of(8 * i, 8), 8)
        grads = [gconv[at, COLS * r : COLS * r + COLS] for r in range(ROWS)]
        for b in range(TAPS):
            moved = extended_rows(own_rows, ext, halo, at, b, lane)
            back = [turned(g, 6 - b) for g in grads]
            for a in range(TAPS):
                terms = back[0] * moved[a]
                for r in range(1, ROWS):
                    terms = terms + back[r] * moved[r + a]
                terms_ref[7 * a + b, at, :] = terms
        return 0

    lax.fori_loop(0, CH // 8, block, 0)
    ones = jnp.ones((2 * COLS, COLS), bf16)
    wide_lane = lax.broadcasted_iota(jnp.int32, (CH, COLS), 1)
    found = jnp.zeros((CH, COLS), f32)
    for k in range(TAPS * TAPS):
        terms = terms_ref[k]
        high = terms.astype(bf16)
        low = (terms - high.astype(f32)).astype(bf16)
        both = jnp.concatenate([high, low], axis=1)
        total = jnp.dot(both, ones, preferred_element_type=f32)
        found = jnp.where(wide_lane == 32 + k, total, found)
    blank = jnp.zeros((8, 96), f32)

    def pack(halves):
        for t in range(CHUNKS * SUB):
            source, at = (in_ref, t) if t < TILES_IN else (out_ref, t - TILES_IN)
            i, l = at // 7, at % 7
            if i >= CH // 8:
                tile = jnp.zeros((8, COLS), f32)
            elif l < 6:
                tile = source[8 * i : 8 * i + 8, COLS * l : COLS * l + COLS]
            else:
                tile = jnp.concatenate([source[8 * i : 8 * i + 8, 6 * COLS : HID], blank], axis=1)
                if t < TILES_IN:
                    tile = jnp.where(lane < 32, tile, found[8 * i : 8 * i + 8, :])
            chunk, at = t // SUB, 8 * (t % SUB)
            halves[chunk // 16][chunk % 16, at : at + 8, :] = tile

    pl.when(me[0] == 0)(lambda: pack((keep, send)))
    pl.when(me[0] == 1)(lambda: pack((send, keep)))


def backward_conv(me, gn, cen, inv, own_rows, ext, halo, coef, part_in, part_out):
    smem = pl.BlockSpec(memory_space=pltpu.SMEM)
    vmem = pl.BlockSpec(memory_space=pltpu.VMEM)
    return pl.pallas_call(
        grad_kernel,
        out_shape=[jax.ShapeDtypeStruct((CHUNKS // 2, 8 * SUB, COLS), f32)] * 2,
        in_specs=[smem] + [vmem] * 9,
        out_specs=[vmem] * 2,
        scratch_shapes=[
            pltpu.VMEM((CH, CELLS), f32),
            pltpu.VMEM((TAPS * TAPS, CH, COLS), f32),
        ],
        compiler_params=pltpu.CompilerParams(vmem_limit_bytes=BIG),
        name="backward_conv",
    )(me, gn, cen, inv, own_rows, ext, halo, coef, part_in, part_out)


def unpack_kernel(me, own_half, other_half, in_ref, out_ref, k_ref, taps):
    share = 1.0 / (8 * TILES * CH * CELLS)

    def spread(halves):
        for chunk in range(CHUNKS):
            values = halves[chunk // 16][chunk % 16].astype(f32) * share
            for p in range(SUB):
                t = SUB * chunk + p
                dest, at = (in_ref, t) if t < TILES_IN else (out_ref, t - TILES_IN)
                i, l = at // 7, at % 7
                tile = values[8 * p : 8 * p + 8, :]
                if i >= CH // 8:
                    continue
                if l < 6:
                    dest[8 * i : 8 * i + 8, COLS * l : COLS * l + COLS] = tile
                else:
                    dest[8 * i : 8 * i + 8, 6 * COLS : HID] = tile[:, 0:32]
                    if t < TILES_IN:
                        taps[8 * i : 8 * i + 8, :] = tile

    pl.when(me[0] == 0)(lambda: spread((own_half, other_half)))
    pl.when(me[0] == 1)(lambda: spread((other_half, own_half)))
    taps[CH:256, :] = jnp.zeros((256 - CH, COLS), f32)
    k_ref[...] = jnp.transpose(taps[...])[32:81, 0:CH]


def unpack(me, own_half, other_half):
    vmem = pl.BlockSpec(memory_space=pltpu.VMEM)
    return pl.pallas_call(
        unpack_kernel,
        out_shape=[
            jax.ShapeDtypeStruct((CH, HID), f32),
            jax.ShapeDtypeStruct((CH, HID), f32),
            jax.ShapeDtypeStruct((49, CH), f32),
        ],
        in_specs=[pl.BlockSpec(memory_space=pltpu.SMEM), vmem, vmem],
        out_specs=[vmem] * 3,
        scratch_shapes=[pltpu.VMEM((256, COLS), f32)],
        compiler_params=pltpu.CompilerParams(vmem_limit_bytes=BIG),
        name="unpack",
    )(me, own_half, other_half)


def swap(values, axis, bits):
    size = lax.axis_size(axis)
    return lax.ppermute(values, axis, [(i, i ^ bits) for i in range(size)])


def reduce_all(keep, send):
    held = keep + swap(send, "core", 1)
    parts = lax.all_to_all(held.astype(bf16), ("x", "y"), 0, 0, tiled=True)
    held = jnp.sum(parts.astype(f32), axis=0)
    copies = jnp.broadcast_to(held.astype(bf16)[None], (8, 8 * SUB, COLS))
    parts = lax.all_to_all(copies, ("zl", "zh"), 0, 0, tiled=True)
    held = jnp.sum(parts.astype(f32), axis=0)
    copies = jnp.broadcast_to(held.astype(bf16)[None], (16, 8 * SUB, COLS))
    half = lax.all_to_all(copies, ("x", "y"), 0, 0, tiled=True)
    return half, swap(half, "core", 1)


def local(
    fields,
    target,
    wet_levels,
    tile_links,
    tile_owner,
    kernel,
    norm_gain,
    weight_in,
    weight_out,
    layer_scale,
):
    own_slot = lax.axis_index(ROUTE).astype(jnp.int32).reshape(1)
    me = lax.axis_index("core").astype(jnp.int32).reshape(1)
    place = (tile_owner & 1) * 16 + ((tile_owner >> 1) & 3) * 4 + (tile_owner >> 3)
    table = jnp.concatenate([tile_links, place[:, None]], axis=1)
    level_of = jnp.arange(CH, dtype=jnp.int32) * LEVELS // CH
    payload = mask_fields(fields[0, 0], wet_levels[0])
    coef = jnp.concatenate([kernel, norm_gain[:, None], layer_scale[:, None]], axis=1)

    own_rows, wide, flat_masked, turn, fold = prepare(table, own_slot, payload, coef)
    chunks = lax.all_to_all(payload.reshape(TILES, PARTS, ROWS, COLS), ROUTE, 0, 0, tiled=True)
    rims = lax.all_to_all(compose(table, chunks), ROUTE, 0, 0, tiled=True)
    rims = rims.reshape(TILES * PARTS, ROWS, COLS)
    centred, flat_norm, inv_std, ext, halo = forward_conv(own_rows, wide, rims, coef, turn, fold)

    scale_wide = layer_scale[:, None]
    hidden = jnp.einsum("ch,cp->hp", weight_in, flat_norm, preferred_element_type=f32)
    activated = gelu_value(hidden).astype(bf16)
    mlp_out = jnp.einsum("hc,hp->cp", weight_out, activated, preferred_element_type=f32)
    block_out = (flat_masked.astype(f32) + scale_wide * mlp_out).astype(bf16)
    flat_wet = wet_levels[0].reshape(1, CELLS) > level_of[:, None]
    misfit = jnp.where(
        flat_wet, block_out.astype(f32) - target[0, 0].reshape(CH, CELLS).astype(f32), 0.0
    )
    grad_mlp = (2.0 * scale_wide * misfit).astype(bf16)
    part_out = jnp.einsum("cp,hp->ch", grad_mlp, activated, preferred_element_type=f32)
    grad_act = jnp.einsum("hc,cp->hp", weight_out, grad_mlp, preferred_element_type=f32)
    grad_hidden = (grad_act * gelu_slope(hidden)).astype(bf16)
    part_in = jnp.einsum("cp,hp->ch", flat_norm, grad_hidden, preferred_element_type=f32)
    grad_normed = jnp.einsum("ch,hp->cp", weight_in, grad_hidden, preferred_element_type=f32)

    keep, send = backward_conv(
        me, grad_normed, centred, inv_std, own_rows, ext, halo, coef, part_in, part_out
    )
    grad_in, grad_out, grad_taps = unpack(me, *reduce_all(keep, send))
    return block_out.reshape(1, 1, CH, ROWS, COLS), grad_in, grad_out.T, grad_taps.T


def solution(mesh):
    fine = Mesh(mesh.devices.reshape(4, 2, 4, 4, 2), ("y", "zh", "zl", "x", "core"))
    big = P(("y", "zh"), TILE, None, None, None)
    placed = (big, big, P(TILE, None, None)) + (P(),) * 7
    return jax.shard_map(
        local,
        mesh=fine,
        in_specs=placed,
        out_specs=(big, P(), P(), P()),
        check_vma=False,
    )
```

```python
import jax
import jax.numpy as jnp
from jax import lax
from jax.experimental import pallas as pl
from jax.experimental.pallas import tpu as pltpu
from jax.sharding import Mesh
from jax.sharding import PartitionSpec as P

LEVELS = 19
TILES = 32
CH = 200
PARTS = 7
ROWS = 8
COLS = 128
EXT = 14
TAPS = 7
HID = 800
CELLS = ROWS * COLS
CHUNKS = 32
SUB = 11
TILES_IN = 175

root_half = 0.7071067811865476
gauss_norm = 0.3989422804014327
norm_epsilon = 1e-06
f32 = jnp.float32
bf16 = jnp.bfloat16
TILE = ("zl", "x", "core")
ROUTE = ("core", "x", "zl")
BIG = 24 << 20


def gelu_value(values):
    return 0.5 * values * (1.0 + lax.erf(values * root_half))


def gelu_slope(values):
    return (
        0.5 * (1.0 + lax.erf(values * root_half))
        + values * jnp.exp(-0.5 * values * values) * gauss_norm
    )


def link_at(table, tile_id, column):
    return jnp.where(tile_id >= 0, table[jnp.maximum(tile_id, 0), column], -1)


def compose_kernel(table, x_ref, o_ref, inverse):
    shape = (PARTS, ROWS, COLS)
    row = lax.broadcasted_iota(jnp.int32, shape, 1)
    lane = lax.broadcasted_iota(jnp.int32, shape, 2)
    edge = (lane < 3) | (lane >= COLS - 3)
    east_side = lane < 64

    def note(k, _):
        inverse[table[k, 5]] = k
        return 0

    lax.fori_loop(0, TILES, note, 0)

    def load(tile_id):
        slot = jnp.maximum(link_at(table, tile_id, 5), 0)
        block = x_ref[slot].astype(f32)
        return jnp.where(tile_id >= 0, block, 0.0)

    def north_of(tile_id):
        block = load(link_at(table, tile_id, 0))
        return jnp.where(link_at(table, tile_id, 4) == 1, pltpu.roll(block, 3, 1), block)

    def body(d, _):
        own = inverse[d]
        west = link_at(table, own, 2)
        east = link_at(table, own, 3)
        north_rows = north_of(own)
        south_rows = load(link_at(table, own, 1))
        sides = jnp.where(edge, jnp.where(east_side, load(east), load(west)), 0.0)
        north_side = (lane < 64) != (link_at(table, own, 4) == 1)
        north_corner = jnp.where(north_side, north_of(east), north_of(west))
        south_corner = jnp.where(
            east_side, load(link_at(table, east, 1)), load(link_at(table, west, 1))
        )
        corners = jnp.where(row < 3, north_corner, south_corner)
        corners = jnp.where(edge & ((row < 3) | (row > 4)), corners, 0.0)
        spread = pltpu.roll(
            sides + pltpu.roll(corners, 64, 2), 24, 2, stride=8, stride_axis=1
        )
        packed = jnp.sum(spread, axis=1, keepdims=True)
        block = jnp.where(row == 3, packed, jnp.where(row < 3, north_rows, south_rows))
        o_ref[d] = block.astype(bf16)
        return 0

    lax.fori_loop(0, TILES, body, 0, unroll=8)


def compose(table, chunks):
    smem = pl.BlockSpec(memory_space=pltpu.SMEM)
    vmem = pl.BlockSpec(memory_space=pltpu.VMEM)
    return pl.pallas_call(
        compose_kernel,
        out_shape=jax.ShapeDtypeStruct((TILES, PARTS, ROWS, COLS), bf16),
        in_specs=[smem, vmem],
        out_specs=vmem,
        scratch_shapes=[pltpu.SMEM((TILES,), jnp.int32)],
        compiler_params=pltpu.CompilerParams(vmem_limit_bytes=BIG),
        name="compose",
    )(table, chunks)


def chosen(center, halo, col_off, lane):
    if col_off < 3:
        return jnp.where(lane >= COLS - 3 + col_off, halo, center)
    if col_off > 3:
        return jnp.where(lane < col_off - 3, halo, center)
    return center


def turned(values, col_off):
    return values if col_off == 3 else pltpu.roll(values, (3 - col_off) % COLS, 1)


def extended_rows(own_rows, ext, halo, at, col_off, lane):
    rows = [ext[r, at, :] for r in range(3)]
    rows += [own_rows[r, at, :] for r in range(ROWS)]
    rows += [ext[r, at, :] for r in range(3, 6)]
    return [chosen(x, halo[r, at, :], col_off, lane) for r, x in enumerate(rows)]


def prepare_kernel(table, own_slot, m_ref, coef, own, taps, flat_ref, turn_ref, fold_ref, mine, wide, sent):

    def widen(i, _):
        taps_of = coef[pl.ds(pl.multiple_of(8 * i, 8), 8), :]
        for k in range(TAPS * TAPS):
            wide[i, k] = jnp.broadcast_to(taps_of[:, k : k + 1], (8, COLS))
        return 0

    lax.fori_loop(0, CH // 8, widen, 0, unroll=5)
    store = pltpu.make_async_copy(wide, taps, sent)
    store.start()
    mine[...] = m_ref[0:CH].astype(f32).reshape(CH * ROWS, COLS)
    for r in range(ROWS):
        values = mine[pl.ds(r, CH, stride=ROWS), :]
        own[r] = values
        flat_ref[:, COLS * r : COLS * r + COLS] = values.astype(bf16)
    slot = own_slot[0]

    def find(k, best):
        return jnp.where(table[k, 5] == slot, k, best)

    fold = table[lax.fori_loop(0, TILES, find, 0), 4] == 1
    row = lax.broadcasted_iota(jnp.int32, (COLS, COLS), 0)
    col = lax.broadcasted_iota(jnp.int32, (COLS, COLS), 1)
    turn_ref[...] = (row == jnp.where(fold, COLS - 1 - col, col)).astype(f32).astype(bf16)
    fold_ref[...] = jnp.broadcast_to(jnp.where(fold, 1, 0), (8, COLS))
    store.wait()


def prepare(table, own_slot, payload, coef):
    smem = pl.BlockSpec(memory_space=pltpu.SMEM)
    vmem = pl.BlockSpec(memory_space=pltpu.VMEM)
    wide = (CH // 8, TAPS * TAPS, 8, COLS)
    return pl.pallas_call(
        prepare_kernel,
        out_shape=[
            jax.ShapeDtypeStruct((ROWS, CH, COLS), f32),
            jax.ShapeDtypeStruct(wide, f32),
            jax.ShapeDtypeStruct((CH, CELLS), bf16),
            jax.ShapeDtypeStruct((COLS, COLS), bf16),
            jax.ShapeDtypeStruct((8, COLS), jnp.int32),
        ],
        in_specs=[smem, smem, vmem, vmem],
        out_specs=[vmem, pl.BlockSpec(memory_space=pltpu.HBM), vmem, vmem, vmem],
        scratch_shapes=[
            pltpu.VMEM((CH * ROWS, COLS), f32),
            pltpu.VMEM(wide, f32),
            pltpu.SemaphoreType.DMA,
        ],
        compiler_params=pltpu.CompilerParams(vmem_limit_bytes=BIG),
        name="prepare",
    )(table, own_slot, payload, coef)


def mask_kernel(fields, wet_levels, o_ref, held, wet_ref, arrived):
    cuts = (0, 56, 104, 152, CH)
    levels = pltpu.make_async_copy(wet_levels, wet_ref, arrived.at[4])
    levels.start()
    copies = []
    for n in range(4):
        span = pl.ds(cuts[n], cuts[n + 1] - cuts[n])
        copies.append(pltpu.make_async_copy(fields.at[span], held.at[span], arrived.at[n]))
        copies[n].start()
    levels.wait()
    wet = wet_ref[...].astype(f32).astype(bf16)
    dry = jnp.zeros((ROWS, COLS), bf16)
    for n in range(4):
        copies[n].wait()
        for c in range(cuts[n], cuts[n + 1]):
            o_ref[c] = jnp.where(wet > bf16(LEVELS * c // CH), held[c], dry)
    o_ref[CH:] = jnp.zeros((TILES * PARTS - CH, ROWS, COLS), bf16)


def mask_fields(fields, wet_levels):
    vmem = pl.BlockSpec(memory_space=pltpu.VMEM)
    return pl.pallas_call(
        mask_kernel,
        out_shape=jax.ShapeDtypeStruct((TILES * PARTS, ROWS, COLS), bf16),
        in_specs=[pl.BlockSpec(memory_space=pltpu.HBM)] * 2,
        out_specs=vmem,
        scratch_shapes=[
            pltpu.VMEM((CH, ROWS, COLS), bf16),
            pltpu.VMEM((ROWS, COLS), jnp.int32),
            pltpu.SemaphoreType.DMA((5,)),
        ],
        compiler_params=pltpu.CompilerParams(vmem_limit_bytes=BIG),
        name="mask_fields",
    )(*(pltpu.with_memory_space_constraint(x, pltpu.HBM) for x in (fields, wet_levels)))


def conv_kernel(
    own_rows, taps, r_ref, coef, turn_ref, fold_ref, cen_ref, norm_ref, inv_ref, ext, halo, rims, wide, arrived
):
    fetches = []
    for p in range(5):
        span = pl.ds(5 * p, 5)
        fetches.append(pltpu.make_async_copy(taps.at[span], wide.at[span], arrived.at[p]))
        fetches[p].start()
    fold = jnp.broadcast_to(fold_ref[0:1, :], (CH, COLS)) == 1
    rims[...] = r_ref[0:CH].astype(f32).reshape(CH * ROWS, COLS)
    turn = turn_ref[...]
    edges = rims[pl.ds(3, CH, stride=ROWS), :]
    for r in range(11):
        halo[r] = edges if r == 0 else pltpu.roll(edges, COLS - 8 * r, 1)
    north = [rims[pl.ds(t, CH, stride=ROWS), :] for t in range(3)]
    corner = [pltpu.roll(edges, COLS - 8 * (11 + t), 1) for t in range(3)]
    for t in range(3):
        ext[t] = rims[pl.ds(5 + t, CH, stride=ROWS), :]
        for dest, source, first in ((ext, north, 3), (halo, corner, 11)):
            raw = jnp.where(fold, source[2 - t], source[t]).astype(bf16)
            dest[first + t] = jnp.dot(raw, turn, preferred_element_type=f32)
    lane = lax.broadcasted_iota(jnp.int32, (8, COLS), 1)

    def block(i, sums):
        at = pl.ds(pl.multiple_of(8 * i, 8), 8)
        acc = [jnp.zeros((8, COLS), f32) for _ in range(ROWS)]
        for b in range(TAPS):
            moved = extended_rows(own_rows, ext, halo, at, b, lane)
            part = [None] * ROWS
            for a in range(TAPS):
                tap = wide[i, 7 * a + b]
                for r in range(ROWS):
                    term = tap * moved[r + a]
                    part[r] = term if a == 0 else part[r] + term
            for r in range(ROWS):
                acc[r] = acc[r] + turned(part[r], b)
        for r in range(ROWS):
            cen_ref[at, COLS * r : COLS * r + COLS] = acc[r]
        return tuple(s + x for s, x in zip(sums, acc))

    sums = tuple(jnp.zeros((8, COLS), f32) for _ in range(ROWS))
    for p in range(5):
        fetches[p].wait()
        sums = lax.fori_loop(5 * p, 5 * p + 5, block, sums)
    gain = jnp.broadcast_to(coef[:, 49:50], (CH, COLS))
    for r in range(ROWS):
        at = slice(COLS * r, COLS * r + COLS)
        mean = jnp.sum(sums[r], axis=0, keepdims=True) * (1.0 / CH)
        off = cen_ref[:, at] - mean
        var = jnp.sum(off * off, axis=0, keepdims=True) * (1.0 / CH)
        inv = 1.0 / jnp.sqrt(var + norm_epsilon)
        centred = off * inv
        cen_ref[:, at] = centred
        norm_ref[:, at] = (centred * gain).astype(bf16)
        inv_ref[r : r + 1, :] = inv


def forward_conv(own_rows, wide, rims, coef, turn, fold):
    vmem = pl.BlockSpec(memory_space=pltpu.VMEM)
    shapes = [
        ((CH, CELLS), f32),
        ((CH, CELLS), bf16),
        ((ROWS, COLS), f32),
        ((6, CH, COLS), f32),
        ((EXT, CH, COLS), f32),
    ]
    return pl.pallas_call(
        conv_kernel,
        out_shape=[jax.ShapeDtypeStruct(s, d) for s, d in shapes],
        in_specs=[vmem, pl.BlockSpec(memory_space=pltpu.HBM), vmem, vmem, vmem, vmem],
        out_specs=[vmem] * len(shapes),
        scratch_shapes=[
            pltpu.VMEM((CH * ROWS, COLS), f32),
            pltpu.VMEM((CH // 8, TAPS * TAPS, 8, COLS), f32),
            pltpu.SemaphoreType.DMA((5,)),
        ],
        compiler_params=pltpu.CompilerParams(vmem_limit_bytes=BIG),
        name="forward_conv",
    )(own_rows, pltpu.with_memory_space_constraint(wide, pltpu.HBM), rims, coef, turn, fold)


def grad_kernel(
    me, gn_ref, cen_ref, inv_ref, own_rows, ext, halo, coef, in_ref, out_ref, keep, send, gconv, terms_ref
):
    gain = jnp.broadcast_to(coef[:, 49:50], (CH, COLS))
    for r in range(ROWS):
        at = slice(COLS * r, COLS * r + COLS)
        scaled = gn_ref[:, at] * gain
        centred = cen_ref[:, at]
        mean = jnp.sum(scaled, axis=0, keepdims=True) * (1.0 / CH)
        along = jnp.sum(scaled * centred, axis=0, keepdims=True) * (1.0 / CH)
        gconv[:, at] = (scaled - mean - centred * along) * inv_ref[r : r + 1, :]
    lane = lax.broadcasted_iota(jnp.int32, (8, COLS), 1)

    def block(i, _):
        at = pl.ds(pl.multiple_of(8 * i, 8), 8)
        grads = [gconv[at, COLS * r : COLS * r + COLS] for r in range(ROWS)]
        for b in range(TAPS):
            moved = extended_rows(own_rows, ext, halo, at, b, lane)
            back = [turned(g, 6 - b) for g in grads]
            for a in range(TAPS):
                terms = back[0] * moved[a]
                for r in range(1, ROWS):
                    terms = terms + back[r] * moved[r + a]
                terms_ref[7 * a + b, at, :] = terms
        return 0

    lax.fori_loop(0, CH // 8, block, 0)
    ones = jnp.ones((COLS, COLS), bf16)
    wide_lane = lax.broadcasted_iota(jnp.int32, (CH, COLS), 1)
    found = jnp.zeros((CH, COLS), f32)
    for k in range(TAPS * TAPS):
        total = jnp.dot(terms_ref[k].astype(bf16), ones, preferred_element_type=f32)
        found = jnp.where(wide_lane == 32 + k, total, found)
    blank = jnp.zeros((8, 96), f32)

    def pack(halves):
        for t in range(CHUNKS * SUB):
            source, at = (in_ref, t) if t < TILES_IN else (out_ref, t - TILES_IN)
            i, l = at // 7, at % 7
            if i >= CH // 8:
                tile = jnp.zeros((8, COLS), f32)
            elif l < 6:
                tile = source[8 * i : 8 * i + 8, COLS * l : COLS * l + COLS]
            else:
                tile = jnp.concatenate([source[8 * i : 8 * i + 8, 6 * COLS : HID], blank], axis=1)
                if t < TILES_IN:
                    tile = jnp.where(lane < 32, tile, found[8 * i : 8 * i + 8, :])
            chunk, at = t // SUB, 8 * (t % SUB)
            halves[chunk // 16][chunk % 16, at : at + 8, :] = tile

    pl.when(me[0] == 0)(lambda: pack((keep, send)))
    pl.when(me[0] == 1)(lambda: pack((send, keep)))


def backward_conv(me, gn, cen, inv, own_rows, ext, halo, coef, part_in, part_out):
    smem = pl.BlockSpec(memory_space=pltpu.SMEM)
    vmem = pl.BlockSpec(memory_space=pltpu.VMEM)
    return pl.pallas_call(
        grad_kernel,
        out_shape=[jax.ShapeDtypeStruct((CHUNKS // 2, 8 * SUB, COLS), f32)] * 2,
        in_specs=[smem] + [vmem] * 9,
        out_specs=[vmem] * 2,
        scratch_shapes=[
            pltpu.VMEM((CH, CELLS), f32),
            pltpu.VMEM((TAPS * TAPS, CH, COLS), f32),
        ],
        compiler_params=pltpu.CompilerParams(vmem_limit_bytes=BIG),
        name="backward_conv",
    )(me, gn, cen, inv, own_rows, ext, halo, coef, part_in, part_out)


def unpack_kernel(me, own_half, other_half, in_ref, out_ref, k_ref, taps):
    share = 1.0 / (8 * TILES * CH * CELLS)

    def spread(halves):
        for chunk in range(CHUNKS):
            values = halves[chunk // 16][chunk % 16].astype(f32) * share
            for p in range(SUB):
                t = SUB * chunk + p
                dest, at = (in_ref, t) if t < TILES_IN else (out_ref, t - TILES_IN)
                i, l = at // 7, at % 7
                tile = values[8 * p : 8 * p + 8, :]
                if i >= CH // 8:
                    continue
                if l < 6:
                    dest[8 * i : 8 * i + 8, COLS * l : COLS * l + COLS] = tile
                else:
                    dest[8 * i : 8 * i + 8, 6 * COLS : HID] = tile[:, 0:32]
                    if t < TILES_IN:
                        taps[8 * i : 8 * i + 8, :] = tile

    pl.when(me[0] == 0)(lambda: spread((own_half, other_half)))
    pl.when(me[0] == 1)(lambda: spread((other_half, own_half)))
    taps[CH:256, :] = jnp.zeros((256 - CH, COLS), f32)
    k_ref[...] = jnp.transpose(taps[...])[32:81, 0:CH]


def unpack(me, own_half, other_half):
    vmem = pl.BlockSpec(memory_space=pltpu.VMEM)
    return pl.pallas_call(
        unpack_kernel,
        out_shape=[
            jax.ShapeDtypeStruct((CH, HID), f32),
            jax.ShapeDtypeStruct((CH, HID), f32),
            jax.ShapeDtypeStruct((49, CH), f32),
        ],
        in_specs=[pl.BlockSpec(memory_space=pltpu.SMEM), vmem, vmem],
        out_specs=[vmem] * 3,
        scratch_shapes=[pltpu.VMEM((256, COLS), f32)],
        compiler_params=pltpu.CompilerParams(vmem_limit_bytes=BIG),
        name="unpack",
    )(me, own_half, other_half)


def swap(values, axis, bits):
    size = lax.axis_size(axis)
    return lax.ppermute(values, axis, [(i, i ^ bits) for i in range(size)])


def reduce_all(keep, send):
    held = keep + swap(send, "core", 1)
    parts = lax.all_to_all(held.astype(bf16), ("x", "y"), 0, 0, tiled=True)
    held = jnp.sum(parts.astype(f32), axis=0)
    copies = jnp.broadcast_to(held.astype(bf16)[None], (8, 8 * SUB, COLS))
    parts = lax.all_to_all(copies, ("zl", "zh"), 0, 0, tiled=True)
    held = jnp.sum(parts.astype(f32), axis=0)
    copies = jnp.broadcast_to(held.astype(bf16)[None], (16, 8 * SUB, COLS))
    half = lax.all_to_all(copies, ("x", "y"), 0, 0, tiled=True)
    return half, swap(half, "core", 1)


def local(
    fields,
    target,
    wet_levels,
    tile_links,
    tile_owner,
    kernel,
    norm_gain,
    weight_in,
    weight_out,
    layer_scale,
):
    own_slot = lax.axis_index(ROUTE).astype(jnp.int32).reshape(1)
    me = lax.axis_index("core").astype(jnp.int32).reshape(1)
    place = (tile_owner & 1) * 16 + ((tile_owner >> 1) & 3) * 4 + (tile_owner >> 3)
    table = jnp.concatenate([tile_links, place[:, None]], axis=1)
    level_of = jnp.arange(CH, dtype=jnp.int32) * LEVELS // CH
    payload = mask_fields(fields[0, 0], wet_levels[0])
    coef = jnp.concatenate([kernel, norm_gain[:, None], layer_scale[:, None]], axis=1)

    own_rows, wide, flat_masked, turn, fold = prepare(table, own_slot, payload, coef)
    chunks = lax.all_to_all(payload.reshape(TILES, PARTS, ROWS, COLS), ROUTE, 0, 0, tiled=True)
    rims = lax.all_to_all(compose(table, chunks), ROUTE, 0, 0, tiled=True)
    rims = rims.reshape(TILES * PARTS, ROWS, COLS)
    centred, flat_norm, inv_std, ext, halo = forward_conv(own_rows, wide, rims, coef, turn, fold)

    scale_wide = layer_scale[:, None]
    hidden = jnp.einsum("ch,cp->hp", weight_in, flat_norm, preferred_element_type=f32)
    activated = gelu_value(hidden).astype(bf16)
    mlp_out = jnp.einsum("hc,hp->cp", weight_out, activated, preferred_element_type=f32)
    block_out = (flat_masked.astype(f32) + scale_wide * mlp_out).astype(bf16)
    flat_wet = wet_levels[0].reshape(1, CELLS) > level_of[:, None]
    misfit = jnp.where(
        flat_wet, block_out.astype(f32) - target[0, 0].reshape(CH, CELLS).astype(f32), 0.0
    )
    grad_mlp = (2.0 * scale_wide * misfit).astype(bf16)
    part_out = jnp.einsum("cp,hp->ch", grad_mlp, activated, preferred_element_type=f32)
    grad_act = jnp.einsum("hc,cp->hp", weight_out, grad_mlp, preferred_element_type=f32)
    grad_hidden = (grad_act * gelu_slope(hidden)).astype(bf16)
    part_in = jnp.einsum("cp,hp->ch", flat_norm, grad_hidden, preferred_element_type=f32)
    grad_normed = jnp.einsum("ch,hp->cp", weight_in, grad_hidden, preferred_element_type=f32)

    keep, send = backward_conv(
        me, grad_normed, centred, inv_std, own_rows, ext, halo, coef, part_in, part_out
    )
    grad_in, grad_out, grad_taps = unpack(me, *reduce_all(keep, send))
    return block_out.reshape(1, 1, CH, ROWS, COLS), grad_in, grad_out.T, grad_taps.T


def solution(mesh):
    fine = Mesh(mesh.devices.reshape(4, 2, 4, 4, 2), ("y", "zh", "zl", "x", "core"))
    big = P(("y", "zh"), TILE, None, None, None)
    placed = (big, big, P(TILE, None, None)) + (P(),) * 7
    return jax.shard_map(
        local,
        mesh=fine,
        in_specs=placed,
        out_specs=(big, P(), P(), P()),
        check_vma=False,
    )
```
